256 devices in a mesh: band: 32 (over x_lo, z, core), domain: 8 (over y, x_hi).
Axes of the slice: x: 4 (x_hi: 2, x_lo: 2; x = x_hi * 2 + x_lo), y: 4, z: 8, core: 2. Of those that a mesh axis runs over, the one named last changes fastest.
Arguments:
- orbitals: float32 [512, 64, 4096], P('band', 'domain'), may hold values from -6 to 6
- previous: float32 [512, 64, 4096], P('band', 'domain'), may hold values from -6 to 6
- potential: float32 [64, 4096], P('domain'), may hold values from -3 to 3
- rotation: float32 [512, 512], P(None, 'band'), may hold values from -1 to 1
- accumulated: float32 [512, 64, 4096], P('band', 'domain'), may hold values from -6 to 6
- panel: int32 [1], replicated, may hold values from 0 to 131071
Outputs:
- filtered: float32 [512, 64, 4096], P('band', 'domain')
- rotated: float32 [512, 64, 4096], P('band', 'domain')
The draws below stay inside these ranges and needn't reach their ends.
All inputs are finite; a program needn't handle non-finite values.
Results may differ from the reference program's by a relative error of at most 0.000059.
Values sent between devices are 32-bit elements; how exact they have to be, the bound alone decides.
No kernel may reach another device: no remote copies, remote signals or barrier semaphores. Data moves between devices by JAX's collectives and lax.ppermute only.
A program may use at most 192 MiB of HBM per device.

```python
import jax
import jax.numpy as jnp
from jax import lax

ORB_DEV = 16
NY = 64
NX = 64
ORBS = 512
PANEL = 32
NZ = 64
N_BAND = 32


def block_scale(rng, shape, split, low, top_value):
    loudness = 1.0
    for dim, parts in split:
        heights = jax.random.uniform(jax.random.fold_in(jax.random.fold_in(rng, 6), dim), (parts,), jnp.float32, low / len(split), top_value / len(split))
        loudness = loudness * jnp.repeat(jnp.exp(heights), shape[dim] // parts).reshape((-1,) + (1,) * (len(shape) - 1 - dim))
    return loudness


def noise(stream_key, shape, width, limit, pieces=(), dtype=jnp.bfloat16):
    level = block_scale(stream_key, shape, pieces, -0.22, 0.18) if pieces else 1.0
    entries = jax.random.normal(stream_key, shape, jnp.float32) * width * level
    return jnp.minimum(jnp.maximum(entries, -limit), limit).astype(dtype)


def setup_inputs(seed: int = 0) -> dict:
    key_list = jax.random.split(jax.random.key(seed), 7)
    return {
        "orbitals": noise(key_list[0], (ORBS, NZ, NY * NX), 1.0, 6.0, ((0, 32), (1, 8)), jnp.float32),
        "previous": noise(key_list[1], (ORBS, NZ, NY * NX), 1.0, 6.0, ((0, 32), (1, 8)), jnp.float32),
        "potential": jnp.clip(jax.random.uniform(key_list[2], (NZ, NY * NX), jnp.float32, -3.0, 3.0) * block_scale(key_list[2], (NZ, NY * NX), ((0, 8),), -0.4, 0.0), -3.0, 3.0),
        "rotation": noise(key_list[3], (ORBS, ORBS), (2 * ORB_DEV) ** -0.5, 1.0, ((1, 32),), jnp.float32),
        "accumulated": noise(key_list[4], (ORBS, NZ, NY * NX), 1.0, 6.0, ((0, 32), (1, 8)), jnp.float32),
        "panel": jax.random.randint(key_list[5], (1,), 0, N_BAND * 4096).astype(jnp.int32),
    }


coefs = (-5369.0 / 1800.0, 12.0 / 7.0, -15.0 / 56.0, 10.0 / 189.0, -1.0 / 112.0, 2.0 / 1925.0, -1.0 / 16632.0)


def apply_filter(cur, prev, potential):
    lap = 3.0 * coefs[0] * cur
    for step in range(1, 7):
        for axis in (1, 2, 3):
            lap = lap + coefs[step] * (jnp.roll(cur, step, axis) + jnp.roll(cur, -step, axis))
    ham = -2.0 * lap + potential[None] * cur
    return (ham - 36.0 * cur) / 14.0 - prev


def reference(orbitals, previous, potential, rotation, accumulated, panel):
    shape = orbitals.shape
    grid = (NZ, NY, NX)
    cur = orbitals.reshape((N_BAND, ORB_DEV) + grid)
    prev = previous.reshape((N_BAND, ORB_DEV) + grid)
    field = potential.reshape(grid)
    filtered = lax.map(lambda pair: apply_filter(pair[0], pair[1], field), (cur, prev)).reshape(shape)
    which = (panel[0] % (N_BAND // 2)).astype(jnp.int32)
    start = (which * PANEL).astype(jnp.int32)
    block = lax.dynamic_slice_in_dim(filtered, start, PANEL, 0).reshape(PANEL, -1)
    rows = lax.dynamic_slice_in_dim(rotation, start, PANEL, 0)
    product = lax.dot_general(rows, block, (((0,), (0,)), ((), ())), precision=lax.Precision.HIGHEST, preferred_element_type=jnp.float32)
    rotated = accumulated + product.reshape(shape)
    return filtered, rotated
```

```python
import numpy as np
import jax
import jax.numpy as jnp
from jax import lax
from jax.experimental import pallas as pl
from jax.experimental.pallas import tpu as pltpu
from jax.sharding import PartitionSpec as P

coefs = (
    -5369.0 / 1800.0,
    12.0 / 7.0,
    -15.0 / 56.0,
    10.0 / 189.0,
    -1.0 / 112.0,
    2.0 / 1925.0,
    -1.0 / 16632.0,
)
SCALE = -2.0 / 14.0
ROW = 64
LANES = 128
WIDTH = 6
ROWS_X = 2
RING = 8
CORES = 2


def row_matrix():
    out = np.zeros((LANES, LANES))
    for i in range(LANES):
        base = i - i % ROW
        for k in range(1, 7):
            for s in (k, -k):
                out[base + (i + s) % ROW, i] += SCALE * coefs[k]
    return out.astype(np.float32)


def pack_body(orb, head, tail):
    planes = orb.shape[1]
    for t in range(orb.shape[2] // LANES):
        tile = orb[0, :, t * LANES : (t + 1) * LANES]
        head[0, t * WIDTH : (t + 1) * WIDTH, :] = tile[:WIDTH]
        tail[0, t * WIDTH : (t + 1) * WIDTH, :] = tile[planes - WIDTH :]


def pack(orb):
    n, planes, cells = orb.shape
    rows = cells // LANES * WIDTH
    return pl.pallas_call(
        pack_body,
        grid=(n,),
        in_specs=[pl.BlockSpec((1, planes, cells), lambda i: (i, 0, 0))],
        out_specs=[pl.BlockSpec((1, rows, LANES), lambda i: (i, 0, 0))] * 2,
        out_shape=[jax.ShapeDtypeStruct((n, rows, LANES), jnp.float32)] * 2,
        cost_estimate=pl.CostEstimate(flops=0, bytes_accessed=5 * n * planes * cells * 2, transcendentals=0),
    )(orb)


def filter_body(orb, low, high, prev, pot, mat, out, ext, half, rowsum):
    planes = orb.shape[1]
    tiles = orb.shape[2] // LANES
    span = planes + 2 * WIDTH + 4
    lane = lax.broadcasted_iota(jnp.int32, (planes, LANES), 1)
    rolled = None
    first = None
    for t in range(tiles):
        tile = orb[0, :, t * LANES : (t + 1) * LANES]
        ext[span * t + 2 : span * t + 2 + WIDTH, :] = low[0, t * WIDTH : (t + 1) * WIDTH, :]
        ext[span * t + 8 : span * t + 8 + planes, :] = tile
        ext[span * t + 8 + planes : span * t + 8 + planes + WIDTH, :] = high[0, t * WIDTH : (t + 1) * WIDTH, :]
        now = pltpu.roll(tile, ROW, 1)
        if t:
            half[(t - 1) * planes : t * planes, :] = jnp.where(lane < ROW, rolled, now)
        else:
            first = now
        rolled = now
    half[(tiles - 1) * planes : tiles * planes, :] = jnp.where(lane < ROW, rolled, first)
    cells = jnp.concatenate([orb[0, :, t * LANES : (t + 1) * LANES] for t in range(tiles)], axis=0)
    rowsum[...] = jnp.dot(cells, mat[...], precision=lax.Precision.HIGHEST, preferred_element_type=jnp.float32)
    for t in range(tiles):
        base = span * t + 8
        centre = orb[0, :, t * LANES : (t + 1) * LANES]

        def flat(step):
            u = (t + step) % tiles
            return orb[0, :, u * LANES : (u + 1) * LANES]

        def odd(step):
            u = (t + step) % tiles
            return half[u * planes : (u + 1) * planes, :]

        total = rowsum[t * planes : (t + 1) * planes, :]
        for k in range(1, 7):
            pair = ext[base + k : base + k + planes, :] + ext[base - k : base - k + planes, :]
            if k % 2:
                pair = pair + (odd((k - 1) // 2) + odd(-(k + 1) // 2))
            else:
                pair = pair + (flat(k // 2) + flat(-(k // 2)))
            total = total + np.float32(SCALE * coefs[k]) * pair
        diag = pot[:, t * LANES : (t + 1) * LANES] * np.float32(1 / 14.0) + np.float32(3 * SCALE * coefs[0] - 36.0 / 14.0)
        out[0, :, t * LANES : (t + 1) * LANES] = total + diag * centre - prev[0, :, t * LANES : (t + 1) * LANES]


def apply_filter(orb, low, high, prev, pot):
    n, planes, cells = orb.shape
    tiles = cells // LANES
    rows = tiles * WIDTH
    whole = pl.BlockSpec((1, planes, cells), lambda i: (i, 0, 0))
    side = pl.BlockSpec((1, rows, LANES), lambda i: (i, 0, 0))
    return pl.pallas_call(
        filter_body,
        grid=(n,),
        in_specs=[
            whole,
            side,
            side,
            whole,
            pl.BlockSpec((planes, cells), lambda i: (0, 0)),
            pl.BlockSpec((LANES, LANES), lambda i: (0, 0)),
        ],
        out_specs=whole,
        out_shape=jax.ShapeDtypeStruct((n, planes, cells), jnp.float32),
        scratch_shapes=[
            pltpu.VMEM((tiles * (planes + 2 * WIDTH + 4), LANES), jnp.float32),
            pltpu.VMEM((tiles * planes, LANES), jnp.float32),
            pltpu.VMEM((tiles * planes, LANES), jnp.float32),
        ],
        cost_estimate=pl.CostEstimate(
            flops=n * planes * cells * 1600, bytes_accessed=19 * n * planes * cells, transcendentals=0
        ),
    )(orb, low, high, prev, pot, jnp.asarray(row_matrix()))


def panel_body(acc, *rest):
    blocks, (weights, out) = rest[:-2], rest[-2:]
    n, planes, width = acc.shape
    parts = [b[...].reshape(b.shape[0] * planes, width) for b in blocks]
    block = jnp.concatenate(parts, axis=0)
    prod = jnp.dot(weights[...], block, precision=lax.Precision.HIGHEST, preferred_element_type=jnp.float32)
    out[...] = acc[...] + prod.reshape(n, planes, width)


def add_panel(acc, blocks, rows, chunk=512):
    n, planes, cells = acc.shape
    weights = jnp.kron(rows.T, jnp.eye(planes, dtype=jnp.float32))
    spec = lambda m: pl.BlockSpec((m, planes, chunk), lambda i: (0, 0, i))
    k = sum(b.shape[0] for b in blocks)
    return pl.pallas_call(
        panel_body,
        grid=(cells // chunk,),
        in_specs=[spec(n)] + [spec(b.shape[0]) for b in blocks] + [pl.BlockSpec(weights.shape, lambda i: (0, 0))],
        out_specs=spec(n),
        out_shape=jax.ShapeDtypeStruct(acc.shape, jnp.float32),
        cost_estimate=pl.CostEstimate(
            flops=12 * n * planes * planes * k * cells, bytes_accessed=4 * (2 * n + k) * planes * cells, transcendentals=0
        ),
    )(acc, *blocks, weights)


def seat(x, z, core):
    return (x * RING + z % RING) * CORES + core


def everywhere(step):
    return [
        (seat(x, z, c), seat(*step(x, z, c))) for x in range(ROWS_X) for z in range(RING) for c in range(CORES)
    ]


ONWARD = everywhere(lambda x, z, c: (x, z + 1, c))
BACK = everywhere(lambda x, z, c: (x, z - 1, c))
ACROSS = everywhere(lambda x, z, c: (1 - x, z, c))
PARTNER = everywhere(lambda x, z, c: (x, z, 1 - c))


def spread(root, share):
    def run(block):
        got = None
        for step in (4, 3, 5, 2, 6, 1, 7):
            z = (root + step) % RING
            pairs = [(seat(x, root, c), seat(x, z, c)) for x in range(ROWS_X) for c in range(CORES)]
            part = lax.ppermute(block[z * share : (z + 1) * share], "band", pairs)
            got = part if got is None else got + part
        return got

    return run


def local(orbitals, previous, potential, rotation, accumulated, panel):
    count = orbitals.shape[0]
    share = count // RING
    where = lax.axis_index("band")
    x, z, core = where // (RING * CORES), where // CORES % RING, where % CORES
    chip = panel[0] % (ROWS_X * RING)
    root_x, root_z = chip // RING, chip % RING

    head, tail = pack(orbitals)
    size = lax.axis_size("domain")
    low = lax.ppermute(tail, "domain", [(i, (i + 1) % size) for i in range(size)])
    high = lax.ppermute(head, "domain", [((i + 1) % size, i) for i in range(size)])
    filtered = apply_filter(orbitals, low, high, previous, potential)

    got = lax.switch(root_z, [spread(r, share) for r in range(RING)], filtered)
    own = lax.dynamic_slice_in_dim(filtered, z * share, share, 0)
    piece = jnp.where(z == root_z, own, got)
    other = lax.ppermute(piece, "band", ACROSS)
    piece = jnp.where(x == root_x, piece, other)

    blocks = [piece]
    offsets = [(0, 0), (0, 1)]
    up = down = piece
    for step in (1, 2, 3):
        up = lax.ppermute(up, "band", ONWARD)
        down = lax.ppermute(down, "band", BACK)
        blocks += [up, down]
        offsets += [(-step, 0), (-step, 1), (step, 0), (step, 1)]
    half = share // 2
    blocks += [lax.ppermute(up[:half], "band", ONWARD), lax.ppermute(down[half:], "band", BACK)]
    offsets += [(-4, 0), (4, 1)]
    blocks += [lax.ppermute(b, "band", PARTNER) for b in blocks]

    order = jnp.stack([(z + off) % RING * share + o for off, o in offsets])
    order = jnp.concatenate([order + core * count, order + (1 - core) * count])
    rows = lax.dynamic_slice_in_dim(rotation, chip * CORES * count, CORES * count, 0)
    pick = order[:, None] == lax.iota(jnp.int32, CORES * count)[None, :]
    rows = jnp.sum(jnp.where(pick[:, :, None], rows[None], 0.0), axis=1)
    rotated = add_panel(accumulated, blocks, rows)
    return filtered, rotated


def solution(mesh):
    in_specs = (
        P("band", "domain", None),
        P("band", "domain", None),
        P("domain", None),
        P(None, "band"),
        P("band", "domain", None),
        P(),
    )
    out_specs = (P("band", "domain", None), P("band", "domain", None))
    return jax.shard_map(local, mesh=mesh, in_specs=in_specs, out_specs=out_specs, check_vma=False)
```

```python
import numpy as np
import jax
import jax.numpy as jnp
from jax import lax
from jax.experimental import pallas as pl
from jax.experimental.pallas import tpu as pltpu
from jax.sharding import PartitionSpec as P


coefs = (
    -5369.0 / 1800.0,
    12.0 / 7.0,
    -15.0 / 56.0,
    10.0 / 189.0,
    -1.0 / 112.0,
    2.0 / 1925.0,
    -1.0 / 16632.0,
)
SCALE = -2.0 / 14.0
ROW = 64
LANES = 128
WIDTH = 6
ROWS_X = 2
RING = 8
CORES = 2


def row_matrix():
    out = np.zeros((LANES, LANES))
    for i in range(LANES):
        base = i - i % ROW
        for k in range(1, 7):
            for s in (k, -k):
                out[base + (i + s) % ROW, i] += SCALE * coefs[k]
    return out.astype(np.float32)


def mixed(full, spare, limit, below):
    sub = lax.broadcasted_iota(jnp.int32, full.shape, 0)
    return jnp.where(sub < limit, full, spare) if below else jnp.where(sub >= limit, full, spare)


def pack_body(orb, head, tail):
    for i in range(orb.shape[0]):
        for g in range(orb.shape[2] // (4 * LANES)):
            tiles = [orb[i, :, (4 * g + m) * LANES : (4 * g + m + 1) * LANES] for m in range(4)]
            for m in range(3):
                spare = pltpu.roll(tiles[3], 6 - 2 * m, 0)
                span = slice((3 * g + m) * LANES, (3 * g + m + 1) * LANES)
                head[i, :, span] = mixed(tiles[m], spare, WIDTH, True)
                tail[i, :, span] = mixed(tiles[m], spare, 2, False)


def unpacked(side, first):
    out = []
    for g in range(side.shape[2] // (3 * LANES)):
        three = [side[0, :, (3 * g + m) * LANES : (3 * g + m + 1) * LANES] for m in range(3)]
        rolled = [pltpu.roll(v, 2 + 2 * m, 0) for m, v in enumerate(three)]
        last = mixed(rolled[0], mixed(rolled[1], rolled[2], first + 4, True), first + 2, True)
        out += three + [last]
    return out


def pack(orb):
    n, planes, cells = orb.shape
    thin = cells * WIDTH // planes
    step = 2
    return pl.pallas_call(
        pack_body,
        grid=(n // step,),
        in_specs=[pl.BlockSpec((step, planes, cells), lambda i: (i, 0, 0))],
        out_specs=[pl.BlockSpec((step, planes, thin), lambda i: (i, 0, 0))] * 2,
        out_shape=[jax.ShapeDtypeStruct((n, planes, thin), jnp.float32)] * 2,
        cost_estimate=pl.CostEstimate(flops=0, bytes_accessed=10 * n * planes * cells, transcendentals=0),
    )(orb)


def filter_body(orb, low, high, prev, pot, mat, out, ext, half, rowsum):
    planes = orb.shape[1]
    tiles = orb.shape[2] // LANES
    span = 3 * planes
    low_tiles = unpacked(low, 2)
    high_tiles = unpacked(high, 0)
    lane = lax.broadcasted_iota(jnp.int32, (planes, LANES), 1)
    rolled = None
    first = None
    for t in range(tiles):
        tile = orb[0, :, t * LANES : (t + 1) * LANES]
        ext[span * t : span * t + planes, :] = low_tiles[t]
        ext[span * t + planes : span * t + 2 * planes, :] = tile
        ext[span * t + 2 * planes : span * t + 3 * planes, :] = high_tiles[t]
        now = pltpu.roll(tile, ROW, 1)
        if t:
            half[(t - 1) * planes : t * planes, :] = jnp.where(lane < ROW, rolled, now)
        else:
            first = now
        rolled = now
    half[(tiles - 1) * planes : tiles * planes, :] = jnp.where(lane < ROW, rolled, first)
    cells = jnp.concatenate([orb[0, :, t * LANES : (t + 1) * LANES] for t in range(tiles)], axis=0)
    rowsum[...] = jnp.dot(cells, mat[...], precision=lax.Precision.HIGHEST, preferred_element_type=jnp.float32)
    for t in range(tiles):
        base = span * t + planes
        centre = orb[0, :, t * LANES : (t + 1) * LANES]

        def flat(step):
            u = (t + step) % tiles
            return orb[0, :, u * LANES : (u + 1) * LANES]

        def odd(step):
            u = (t + step) % tiles
            return half[u * planes : (u + 1) * planes, :]

        total = rowsum[t * planes : (t + 1) * planes, :]
        for k in range(1, 7):
            pair = ext[base + k : base + k + planes, :] + ext[base - k : base - k + planes, :]
            if k % 2:
                pair = pair + (odd((k - 1) // 2) + odd(-(k + 1) // 2))
            else:
                pair = pair + (flat(k // 2) + flat(-(k // 2)))
            total = total + np.float32(SCALE * coefs[k]) * pair
        diag = pot[:, t * LANES : (t + 1) * LANES] * np.float32(1 / 14.0) + np.float32(3 * SCALE * coefs[0] - 36.0 / 14.0)
        out[0, :, t * LANES : (t + 1) * LANES] = total + diag * centre - prev[0, :, t * LANES : (t + 1) * LANES]


def apply_filter(orb, low, high, prev, pot):
    n, planes, cells = orb.shape
    tiles = cells // LANES
    thin = cells * WIDTH // planes
    whole = pl.BlockSpec((1, planes, cells), lambda i: (i, 0, 0))
    side = pl.BlockSpec((1, planes, thin), lambda i: (i, 0, 0))
    return pl.pallas_call(
        filter_body,
        grid=(n,),
        in_specs=[
            whole,
            side,
            side,
            whole,
            pl.BlockSpec((planes, cells), lambda i: (0, 0)),
            pl.BlockSpec((LANES, LANES), lambda i: (0, 0)),
        ],
        out_specs=whole,
        out_shape=jax.ShapeDtypeStruct((n, planes, cells), jnp.float32),
        scratch_shapes=[
            pltpu.VMEM((tiles * 3 * planes, LANES), jnp.float32),
            pltpu.VMEM((tiles * planes, LANES), jnp.float32),
            pltpu.VMEM((tiles * planes, LANES), jnp.float32),
        ],
        cost_estimate=pl.CostEstimate(
            flops=n * planes * cells * 1600, bytes_accessed=19 * n * planes * cells, transcendentals=0
        ),
    )(orb, low, high, prev, pot, jnp.asarray(row_matrix()))


def panel_body(acc, *rest):
    blocks, (weights, out) = rest[:-2], rest[-2:]
    n, planes, width = acc.shape
    parts = [b[...].reshape(b.shape[0] * planes, width) for b in blocks]
    block = jnp.concatenate(parts, axis=0)
    prod = jnp.dot(weights[...], block, precision=lax.Precision.HIGHEST, preferred_element_type=jnp.float32)
    out[...] = acc[...] + prod.reshape(n, planes, width)


def add_panel(acc, blocks, rows, chunk=512):
    n, planes, cells = acc.shape
    weights = jnp.kron(rows.T, jnp.eye(planes, dtype=jnp.float32))
    spec = lambda m: pl.BlockSpec((m, planes, chunk), lambda i: (0, 0, i))
    k = sum(b.shape[0] for b in blocks)
    return pl.pallas_call(
        panel_body,
        grid=(cells // chunk,),
        in_specs=[spec(n)] + [spec(b.shape[0]) for b in blocks] + [pl.BlockSpec(weights.shape, lambda i: (0, 0))],
        out_specs=spec(n),
        out_shape=jax.ShapeDtypeStruct(acc.shape, jnp.float32),
        cost_estimate=pl.CostEstimate(
            flops=12 * n * planes * planes * k * cells, bytes_accessed=4 * (2 * n + k) * planes * cells, transcendentals=0
        ),
    )(acc, *blocks, weights)


def seat(x, z, core):
    return (x * RING + z % RING) * CORES + core


def everywhere(step):
    return [
        (seat(x, z, c), seat(*step(x, z, c))) for x in range(ROWS_X) for z in range(RING) for c in range(CORES)
    ]


ONWARD = everywhere(lambda x, z, c: (x, z + 1, c))
BACK = everywhere(lambda x, z, c: (x, z - 1, c))
ACROSS = everywhere(lambda x, z, c: (1 - x, z, c))
PARTNER = everywhere(lambda x, z, c: (x, z, 1 - c))


def deal_body(z, block, *hands):
    for i, hand in enumerate(hands):

        @pl.when(pl.program_id(0) == i)
        def _(hand=hand):
            hand[...] = block[...]


def deal(block, z):
    n, planes, cells = block.shape
    share = n // RING
    hand = pl.BlockSpec((share, planes, cells), lambda i, z: (0, 0, 0))
    return pl.pallas_call(
        deal_body,
        grid_spec=pltpu.PrefetchScalarGridSpec(
            num_scalar_prefetch=1,
            grid=(RING,),
            in_specs=[pl.BlockSpec((share, planes, cells), lambda i, z: ((z[0] + i) & (RING - 1), 0, 0))],
            out_specs=[hand] * RING,
        ),
        out_shape=[jax.ShapeDtypeStruct((share, planes, cells), jnp.float32)] * RING,
        cost_estimate=pl.CostEstimate(flops=0, bytes_accessed=8 * n * planes * cells, transcendentals=0),
    )(z[None], block)


def spread(root):
    def run(hands):
        got = [None] * (RING - 1)
        for step, spacing in ((4, 4), (3, 4), (5, 4), (2, 2), (6, 2), (1, 1), (7, 1)):
            pairs = [
                (seat(x, s, c), seat(x, s + step, c))
                for x in range(ROWS_X)
                for s in range(RING)
                if (s - root) % spacing == 0
                for c in range(CORES)
            ]
            got[step - 1] = lax.ppermute(hands[step - 1], "band", pairs)
        return tuple(got)

    return run


def chosen(own, got, offset):
    for i, part in enumerate(got):
        own = jnp.where(offset == i + 1, part, own)
    return own


def halo(head, tail):
    size = lax.axis_size("domain")
    low = lax.ppermute(tail, "domain", [(i, (i + 1) % size) for i in range(size)])
    high = lax.ppermute(head, "domain", [((i + 1) % size, i) for i in range(size)])
    return low, high


def step(orbitals, previous, potential, rotation, accumulated, panel):
    count = orbitals.shape[0]
    share = count // RING
    where = lax.axis_index("band")
    x, z, core = where >> 4, (where >> 1) & 7, where & 1
    chip = panel[0] & (ROWS_X * RING - 1)
    root_x, root_z = chip >> 3, chip & 7

    offset = (z - root_z) & (RING - 1)

    ends = pack(orbitals)
    low, high = halo(*ends)

    mine, *hands = deal(orbitals, z)
    got = lax.switch(root_z & 3, [spread(r) for r in range(4)], hands)
    piece = chosen(mine, got, offset)
    mine, *hands = deal(previous, z)
    (below, above), got = lax.switch(
        root_z & 3, [lambda h, e, r=r: (halo(*e), spread(r)(h)) for r in range(4)], hands, pack(piece)
    )
    before = chosen(mine, got, offset)
    piece = apply_filter(piece, below, above, before, potential)
    other = lax.ppermute(piece, "band", ACROSS)
    piece = jnp.where(x == root_x, piece, other)
    filtered = apply_filter(orbitals, low, high, previous, potential)

    blocks = [piece]
    offsets = [(0, 0), (0, 1)]
    up = down = piece
    for step in (1, 2, 3):
        up = lax.ppermute(up, "band", ONWARD)
        down = lax.ppermute(down, "band", BACK)
        blocks += [up, down]
        offsets += [(-step, 0), (-step, 1), (step, 0), (step, 1)]
    half = share // 2
    blocks += [lax.ppermute(up[:half], "band", ONWARD), lax.ppermute(down[half:], "band", BACK)]
    offsets += [(-4, 0), (4, 1)]
    blocks += [lax.ppermute(b, "band", PARTNER) for b in blocks]

    order = jnp.stack([((z + off) & 7) * share + o for off, o in offsets])
    order = jnp.concatenate([order + core * count, order + (1 - core) * count])
    rows = lax.dynamic_slice_in_dim(rotation, chip * CORES * count, CORES * count, 0)
    pick = order[:, None] == lax.iota(jnp.int32, CORES * count)[None, :]
    rows = jnp.sum(jnp.where(pick[:, :, None], rows[None], 0.0), axis=1)
    rotated = add_panel(accumulated, blocks, rows)
    return filtered, rotated


def solution(mesh):
    in_specs = (
        P("band", "domain", None),
        P("band", "domain", None),
        P("domain", None),
        P(None, "band"),
        P("band", "domain", None),
        P(),
    )
    out_specs = (P("band", "domain", None), P("band", "domain", None))
    return jax.shard_map(step, mesh=mesh, in_specs=in_specs, out_specs=out_specs, check_vma=False)
```

```python
import numpy as np
import jax
import jax.numpy as jnp
from jax import lax
from jax.experimental import pallas as pl
from jax.experimental.pallas import tpu as pltpu
from jax.sharding import PartitionSpec as P


coefs = (
    -5369.0 / 1800.0,
    12.0 / 7.0,
    -15.0 / 56.0,
    10.0 / 189.0,
    -1.0 / 112.0,
    2.0 / 1925.0,
    -1.0 / 16632.0,
)
SCALE = -2.0 / 14.0
ROW = 64
LANES = 128
WIDTH = 6
ROWS_X = 2
RING = 8
CORES = 2


def row_matrix():
    out = np.zeros((LANES, LANES))
    for i in range(LANES):
        base = i - i % ROW
        for k in range(1, 7):
            for s in (k, -k):
                out[base + (i + s) % ROW, i] += SCALE * coefs[k]
    return out.astype(np.float32)


def mixed(full, spare, limit, below):
    sub = lax.broadcasted_iota(jnp.int32, full.shape, 0)
    return jnp.where(sub < limit, full, spare) if below else jnp.where(sub >= limit, full, spare)


def pack_body(orb, head, tail):
    for i in range(orb.shape[0]):
        for g in range(orb.shape[2] // (4 * LANES)):
            tiles = [orb[i, :, (4 * g + m) * LANES : (4 * g + m + 1) * LANES] for m in range(4)]
            for m in range(3):
                spare = pltpu.roll(tiles[3], 6 - 2 * m, 0)
                span = slice((3 * g + m) * LANES, (3 * g + m + 1) * LANES)
                head[i, :, span] = mixed(tiles[m], spare, WIDTH, True)
                tail[i, :, span] = mixed(tiles[m], spare, 2, False)


def unpacked(side, i, first):
    out = []
    for g in range(side.shape[2] // (3 * LANES)):
        three = [side[i, :, (3 * g + m) * LANES : (3 * g + m + 1) * LANES] for m in range(3)]
        rolled = [pltpu.roll(v, 2 + 2 * m, 0) for m, v in enumerate(three)]
        last = mixed(rolled[0], mixed(rolled[1], rolled[2], first + 4, True), first + 2, True)
        out += three + [last]
    return out


def pack(orb):
    n, planes, cells = orb.shape
    thin = cells * WIDTH // planes
    step = min(n, 4)
    return pl.pallas_call(
        pack_body,
        grid=(n // step,),
        in_specs=[pl.BlockSpec((step, planes, cells), lambda i: (i, 0, 0))],
        out_specs=[pl.BlockSpec((step, planes, thin), lambda i: (i, 0, 0))] * 2,
        out_shape=[jax.ShapeDtypeStruct((n, planes, thin), jnp.float32)] * 2,
        cost_estimate=pl.CostEstimate(flops=0, bytes_accessed=10 * n * planes * cells, transcendentals=0),
    )(orb)


def filter_one(i, orb, low, high, prev, pot, mat, out, ext, half, rowsum):
    planes = orb.shape[1]
    tiles = orb.shape[2] // LANES
    span = 3 * planes
    low_tiles = unpacked(low, i, 2)
    high_tiles = unpacked(high, i, 0)
    lane = lax.broadcasted_iota(jnp.int32, (planes, LANES), 1)
    rolled = None
    first = None
    for t in range(tiles):
        tile = orb[i, :, t * LANES : (t + 1) * LANES]
        ext[span * t : span * t + planes, :] = low_tiles[t]
        ext[span * t + planes : span * t + 2 * planes, :] = tile
        ext[span * t + 2 * planes : span * t + 3 * planes, :] = high_tiles[t]
        now = pltpu.roll(tile, ROW, 1)
        if t:
            half[(t - 1) * planes : t * planes, :] = jnp.where(lane < ROW, rolled, now)
        else:
            first = now
        rolled = now
    half[(tiles - 1) * planes : tiles * planes, :] = jnp.where(lane < ROW, rolled, first)
    cells = jnp.concatenate([orb[i, :, t * LANES : (t + 1) * LANES] for t in range(tiles)], axis=0)
    rowsum[...] = jnp.dot(cells, mat[...], precision=lax.Precision.HIGHEST, preferred_element_type=jnp.float32)
    for t in range(tiles):
        base = span * t + planes
        centre = orb[i, :, t * LANES : (t + 1) * LANES]

        def flat(step):
            u = (t + step) % tiles
            return orb[i, :, u * LANES : (u + 1) * LANES]

        def odd(step):
            u = (t + step) % tiles
            return half[u * planes : (u + 1) * planes, :]

        total = rowsum[t * planes : (t + 1) * planes, :]
        for k in range(1, 7):
            pair = ext[base + k : base + k + planes, :] + ext[base - k : base - k + planes, :]
            if k % 2:
                pair = pair + (odd((k - 1) // 2) + odd(-(k + 1) // 2))
            else:
                pair = pair + (flat(k // 2) + flat(-(k // 2)))
            total = total + np.float32(SCALE * coefs[k]) * pair
        diag = pot[:, t * LANES : (t + 1) * LANES] * np.float32(1 / 14.0) + np.float32(3 * SCALE * coefs[0] - 36.0 / 14.0)
        out[i, :, t * LANES : (t + 1) * LANES] = total + diag * centre - prev[i, :, t * LANES : (t + 1) * LANES]


def filter_body(orb, *refs):
    @pl.loop(0, orb.shape[0])
    def _(i):
        filter_one(i, orb, *refs)


def apply_filter(orb, low, high, prev, pot):
    n, planes, cells = orb.shape
    tiles = cells // LANES
    thin = cells * WIDTH // planes
    step = min(n, 4)
    whole = pl.BlockSpec((step, planes, cells), lambda i: (i, 0, 0))
    side = pl.BlockSpec((step, planes, thin), lambda i: (i, 0, 0))
    return pl.pallas_call(
        filter_body,
        grid=(n // step,),
        in_specs=[
            whole,
            side,
            side,
            whole,
            pl.BlockSpec((planes, cells), lambda i: (0, 0)),
            pl.BlockSpec((LANES, LANES), lambda i: (0, 0)),
        ],
        out_specs=whole,
        out_shape=jax.ShapeDtypeStruct((n, planes, cells), jnp.float32),
        scratch_shapes=[
            pltpu.VMEM((tiles * 3 * planes, LANES), jnp.float32),
            pltpu.VMEM((tiles * planes, LANES), jnp.float32),
            pltpu.VMEM((tiles * planes, LANES), jnp.float32),
        ],
        cost_estimate=pl.CostEstimate(
            flops=n * planes * cells * 1600, bytes_accessed=19 * n * planes * cells, transcendentals=0
        ),
    )(orb, low, high, prev, pot, jnp.asarray(row_matrix()))


def weights_body(scalars, rows, plan, high, low):
    z, core, first = scalars[0], scalars[1], scalars[2]
    offset, which, other = plan[0:1, :], plan[1:2, :], plan[2:3, :]
    seat_core = jnp.where(other == 1, 1 - core, core)
    share = plan[3:4, :]
    order = first + ((z + offset) & (RING - 1)) * share + which + seat_core * (RING * share)
    count, span = rows.shape
    columns = order.shape[1]
    planes = high.shape[0] // count
    pick = lax.broadcasted_iota(jnp.int32, (span, columns), 0) == order
    wide = jnp.dot(rows[...], pick.astype(jnp.float32), precision=lax.Precision.HIGHEST, preferred_element_type=jnp.float32)
    row = lax.broadcasted_iota(jnp.int32, (planes, columns), 0)
    col = lax.broadcasted_iota(jnp.int32, (planes, columns), 1)
    same = (col & (planes - 1)) == row
    for j in range(count):
        full = jnp.where(same, wide[j : j + 1, :], 0.0)
        top = full.astype(jnp.bfloat16).astype(jnp.float32)
        high[j * planes : (j + 1) * planes, :] = top
        low[j * planes : (j + 1) * planes, :] = full - top


def weights(rotation, plan, z, core, chip, share, planes):
    turned = rotation.T
    count = turned.shape[0]
    panel = CORES * RING * share
    per = LANES // panel
    table = np.repeat(np.asarray([(o, i, c, share) for o, i, c in plan], np.int32).T, planes, axis=1)
    table = np.concatenate([table, np.zeros((8 - table.shape[0], table.shape[1]), np.int32)])
    scalars = jnp.stack([z, core, (chip % per) * panel, chip // per])
    shape = (count * planes, table.shape[1])
    return pl.pallas_call(
        weights_body,
        grid_spec=pltpu.PrefetchScalarGridSpec(
            num_scalar_prefetch=1,
            grid=(1,),
            in_specs=[
                pl.BlockSpec((count, LANES), lambda i, s: (0, s[3])),
                pl.BlockSpec(table.shape, lambda i, s: (0, 0)),
            ],
            out_specs=[pl.BlockSpec(shape, lambda i, s: (0, 0))] * 2,
        ),
        out_shape=[jax.ShapeDtypeStruct(shape, jnp.float32)] * 2,
        cost_estimate=pl.CostEstimate(flops=10**6, bytes_accessed=10**6, transcendentals=0),
    )(scalars, turned, jnp.asarray(table))


def panel_body(acc, *rest):
    blocks, (high, low, out) = rest[:-3], rest[-3:]
    n, planes, width = acc.shape
    block = jnp.concatenate([b[...].reshape(b.shape[0] * planes, width) for b in blocks], axis=0)
    block_high = block.astype(jnp.bfloat16)
    block_low = (block - block_high.astype(jnp.float32)).astype(jnp.bfloat16)
    high = high[...].astype(jnp.bfloat16)
    low = low[...].astype(jnp.bfloat16)
    dot = lambda a, b: jnp.dot(a, b, preferred_element_type=jnp.float32)
    prod = dot(high, block_high) + (dot(high, block_low) + dot(low, block_high))
    out[...] = acc[...] + prod.reshape(n, planes, width)


def add_panel(acc, blocks, high, low):
    n, planes, cells = acc.shape
    chunk = cells // 4
    spec = lambda m: pl.BlockSpec((m, planes, chunk), lambda i: (0, 0, i))
    k = sum(b.shape[0] for b in blocks)
    full = pl.BlockSpec(high.shape, lambda i: (0, 0))
    return pl.pallas_call(
        panel_body,
        grid=(cells // chunk,),
        in_specs=[spec(n)] + [spec(b.shape[0]) for b in blocks] + [full, full],
        out_specs=spec(n),
        out_shape=jax.ShapeDtypeStruct(acc.shape, jnp.float32),
        cost_estimate=pl.CostEstimate(
            flops=6 * n * planes * planes * k * cells, bytes_accessed=4 * (2 * n + k) * planes * cells, transcendentals=0
        ),
    )(acc, *blocks, high, low)


def seat(x, z, core):
    return (x * RING + z % RING) * CORES + core


def everywhere(step):
    return [
        (seat(x, z, c), seat(*step(x, z, c))) for x in range(ROWS_X) for z in range(RING) for c in range(CORES)
    ]


ONWARD = everywhere(lambda x, z, c: (x, z + 1, c))
BACK = everywhere(lambda x, z, c: (x, z - 1, c))
ACROSS = everywhere(lambda x, z, c: (1 - x, z, c))
PARTNER = everywhere(lambda x, z, c: (x, z, 1 - c))


def deal_body(z, block, *hands):
    for i, hand in enumerate(hands):
        share = hand.shape[0]
        for m in range(share):
            hand[m] = block[((z[0] + i) & (RING - 1)) * share + m]


def deal(block, z):
    n, planes, cells = block.shape
    share = n // RING
    hand = pl.BlockSpec((share, planes, cells), lambda i, z: (0, 0, 0))
    return pl.pallas_call(
        deal_body,
        grid_spec=pltpu.PrefetchScalarGridSpec(
            num_scalar_prefetch=1,
            grid=(1,),
            in_specs=[pl.BlockSpec(block.shape, lambda i, z: (0, 0, 0))],
            out_specs=[hand] * RING,
        ),
        out_shape=[jax.ShapeDtypeStruct((share, planes, cells), jnp.float32)] * RING,
        cost_estimate=pl.CostEstimate(flops=0, bytes_accessed=8 * n * planes * cells, transcendentals=0),
    )(z[None], block)


def relay(hands, offset):
    share = hands[0].shape[0]
    half = share // 2
    root = offset == 0
    up = lax.ppermute(hands[4][:half], "band", ONWARD)
    down = lax.ppermute(hands[4][half:], "band", BACK)
    up, down = jnp.concatenate([up, up]), jnp.concatenate([down, down])
    for step in (3, 2, 1):
        up = jnp.where(root, hands[step], up)
        down = jnp.where(root, hands[RING - step], down)
        up = lax.ppermute(up, "band", ONWARD)
        down = lax.ppermute(down, "band", BACK)
    middle = jnp.concatenate([up[:half], down[:half]])
    far = jnp.where(offset < 4, up, jnp.where(offset == 4, middle, down))
    return jnp.where(root, hands[0], far)


def halo(head, tail):
    size = lax.axis_size("domain")
    low = lax.ppermute(tail, "domain", [(i, (i + 1) % size) for i in range(size)])
    high = lax.ppermute(head, "domain", [((i + 1) % size, i) for i in range(size)])
    return low, high


def step(orbitals, previous, potential, rotation, accumulated, panel):
    count = orbitals.shape[0]
    share = count // RING
    where = lax.axis_index("band")
    x, z, core = where >> 4, (where >> 1) & 7, where & 1
    chip = panel[0] & (ROWS_X * RING - 1)
    root_x, root_z = chip >> 3, chip & 7

    offset = (z - root_z) & (RING - 1)

    hands = deal(orbitals, z)
    ends = pack(orbitals)
    low, high = halo(*ends)
    hands_before = deal(previous, z)
    piece = relay(hands, offset)
    before = relay(hands_before, offset)
    ends = pack(piece)
    below, above = halo(*ends)
    piece = apply_filter(piece, below, above, before, potential)
    other = lax.ppermute(piece, "band", ACROSS)
    piece = jnp.where(x == root_x, piece, other)
    filtered = apply_filter(orbitals, low, high, previous, potential)

    blocks = [piece]
    plan = [(0, 0), (0, 1)]
    up = down = piece
    for hop in (1, 2, 3):
        up = lax.ppermute(up, "band", ONWARD)
        down = lax.ppermute(down, "band", BACK)
        blocks += [up, down]
        plan += [(-hop, 0), (-hop, 1), (hop, 0), (hop, 1)]
    blocks += [lax.ppermute(up, "band", ONWARD)]
    plan += [(-4, 0), (-4, 1)]
    blocks += [lax.ppermute(b, "band", PARTNER) for b in blocks]
    plan = [(o, i, c) for c in range(CORES) for o, i in plan]
    coefficients = weights(rotation, plan, z, core, chip, share, orbitals.shape[1])
    rotated = add_panel(accumulated, blocks, *coefficients)
    return filtered, rotated


def solution(mesh):
    in_specs = (
        P("band", "domain", None),
        P("band", "domain", None),
        P("domain", None),
        P(None, "band"),
        P("band", "domain", None),
        P(),
    )
    out_specs = (P("band", "domain", None), P("band", "domain", None))
    return jax.shard_map(step, mesh=mesh, in_specs=in_specs, out_specs=out_specs, check_vma=False)
```

```python
import numpy as np
import jax
import jax.numpy as jnp
from jax import lax
from jax.experimental import pallas as pl
from jax.experimental.pallas import tpu as pltpu
from jax.sharding import PartitionSpec as P


coefs = (
    -5369.0 / 1800.0,
    12.0 / 7.0,
    -15.0 / 56.0,
    10.0 / 189.0,
    -1.0 / 112.0,
    2.0 / 1925.0,
    -1.0 / 16632.0,
)
SCALE = -2.0 / 14.0
ROW = 64
LANES = 128
WIDTH = 6
ROWS_X = 2
RING = 8
CORES = 2


def room(mib):
    return pltpu.CompilerParams(vmem_limit_bytes=mib << 20)


def row_matrix():
    out = np.zeros((LANES, LANES))
    for i in range(LANES):
        base = i - i % ROW
        for k in range(1, 7):
            for s in (k, -k):
                out[base + (i + s) % ROW, i] += SCALE * coefs[k]
    return out.astype(np.float32)


def mixed(full, spare, limit, below):
    sub = lax.broadcasted_iota(jnp.int32, full.shape, 0)
    return jnp.where(sub < limit, full, spare) if below else jnp.where(sub >= limit, full, spare)


def pack_body(orb, head, tail):
    for i in range(orb.shape[0]):
        for g in range(orb.shape[2] // (4 * LANES)):
            tiles = [orb[i, :, (4 * g + m) * LANES : (4 * g + m + 1) * LANES] for m in range(4)]
            for m in range(3):
                spare = pltpu.roll(tiles[3], 6 - 2 * m, 0)
                span = slice((3 * g + m) * LANES, (3 * g + m + 1) * LANES)
                head[i, :, span] = mixed(tiles[m], spare, WIDTH, True)
                tail[i, :, span] = mixed(tiles[m], spare, 2, False)


def unpacked(side, i, first):
    out = []
    for g in range(side.shape[2] // (3 * LANES)):
        three = [side[i, :, (3 * g + m) * LANES : (3 * g + m + 1) * LANES] for m in range(3)]
        rolled = [pltpu.roll(v, 2 + 2 * m, 0) for m, v in enumerate(three)]
        last = mixed(rolled[0], mixed(rolled[1], rolled[2], first + 4, True), first + 2, True)
        out += three + [last]
    return out


def pack(orb, first=0, n=None):
    n = n or orb.shape[0]
    planes, cells = orb.shape[1:]
    thin = cells * WIDTH // planes
    step = min(n, 4)
    return pl.pallas_call(
        pack_body,
        grid=(n // step,),
        in_specs=[pl.BlockSpec((step, planes, cells), lambda i: (i + first // step, 0, 0))],
        out_specs=[pl.BlockSpec((step, planes, thin), lambda i: (i, 0, 0))] * 2,
        out_shape=[jax.ShapeDtypeStruct((n, planes, thin), jnp.float32)] * 2,
        compiler_params=room(8),
        cost_estimate=pl.CostEstimate(flops=0, bytes_accessed=10 * n * planes * cells, transcendentals=0),
    )(orb)


def filter_one(i, orb, low, high, prev, pot, mat, out, ext, half, rowsum):
    planes = orb.shape[1]
    tiles = orb.shape[2] // LANES
    span = 3 * planes
    low_tiles = unpacked(low, i, 2)
    high_tiles = unpacked(high, i, 0)
    lane = lax.broadcasted_iota(jnp.int32, (planes, LANES), 1)
    rolled = None
    first = None
    for t in range(tiles):
        tile = orb[i, :, t * LANES : (t + 1) * LANES]
        ext[span * t : span * t + planes, :] = low_tiles[t]
        ext[span * t + planes : span * t + 2 * planes, :] = tile
        ext[span * t + 2 * planes : span * t + 3 * planes, :] = high_tiles[t]
        now = pltpu.roll(tile, ROW, 1)
        if t:
            half[(t - 1) * planes : t * planes, :] = jnp.where(lane < ROW, rolled, now)
        else:
            first = now
        rolled = now
    half[(tiles - 1) * planes : tiles * planes, :] = jnp.where(lane < ROW, rolled, first)
    cells = jnp.concatenate([orb[i, :, t * LANES : (t + 1) * LANES] for t in range(tiles)], axis=0)
    rowsum[...] = jnp.dot(cells, mat[...], precision=lax.Precision.HIGHEST, preferred_element_type=jnp.float32)
    for t in range(tiles):
        base = span * t + planes
        centre = orb[i, :, t * LANES : (t + 1) * LANES]

        def flat(step):
            u = (t + step) % tiles
            return orb[i, :, u * LANES : (u + 1) * LANES]

        def odd(step):
            u = (t + step) % tiles
            return half[u * planes : (u + 1) * planes, :]

        total = rowsum[t * planes : (t + 1) * planes, :]
        for k in range(1, 7):
            pair = ext[base + k : base + k + planes, :] + ext[base - k : base - k + planes, :]
            if k % 2:
                pair = pair + (odd((k - 1) // 2) + odd(-(k + 1) // 2))
            else:
                pair = pair + (flat(k // 2) + flat(-(k // 2)))
            total = total + np.float32(SCALE * coefs[k]) * pair
        diag = pot[:, t * LANES : (t + 1) * LANES] * np.float32(1 / 14.0) + np.float32(3 * SCALE * coefs[0] - 36.0 / 14.0)
        out[i, :, t * LANES : (t + 1) * LANES] = total + diag * centre - prev[i, :, t * LANES : (t + 1) * LANES]


def filter_body(orb, low, high, prev, pot, mat, *rest):
    @pl.loop(0, orb.shape[0])
    def _(i):
        filter_one(i, orb, low, high, prev, pot, mat, *rest[-4:])


def apply_filter(orb, low, high, prev, pot, first=0, into=None):
    total, planes, cells = orb.shape
    n = low.shape[0]
    tiles = cells // LANES
    thin = cells * WIDTH // planes
    step = min(n, 4)
    whole = pl.BlockSpec((step, planes, cells), lambda i: (i + first // step, 0, 0))
    side = pl.BlockSpec((step, planes, thin), lambda i: (i, 0, 0))
    args = [orb, low, high, prev, pot, jnp.asarray(row_matrix())]
    specs = [
        whole,
        side,
        side,
        whole,
        pl.BlockSpec((planes, cells), lambda i: (0, 0)),
        pl.BlockSpec((LANES, LANES), lambda i: (0, 0)),
    ]
    if into is not None:
        args.append(into)
        specs.append(pl.BlockSpec(memory_space=pl.ANY))
    return pl.pallas_call(
        filter_body,
        grid=(n // step,),
        in_specs=specs,
        out_specs=whole,
        out_shape=jax.ShapeDtypeStruct((total, planes, cells), jnp.float32),
        input_output_aliases={} if into is None else {6: 0},
        scratch_shapes=[
            pltpu.VMEM((tiles * 3 * planes, LANES), jnp.float32),
            pltpu.VMEM((tiles * planes, LANES), jnp.float32),
            pltpu.VMEM((tiles * planes, LANES), jnp.float32),
        ],
        compiler_params=room(14),
        cost_estimate=pl.CostEstimate(
            flops=n * planes * cells * 1600, bytes_accessed=19 * n * planes * cells, transcendentals=0
        ),
    )(*args)


def weights_body(scalars, rows, plan, high, low):
    z, core, first = scalars[0], scalars[1], scalars[2]
    offset, which, other = plan[0:1, :], plan[1:2, :], plan[2:3, :]
    seat_core = jnp.where(other == 1, 1 - core, core)
    share = plan[3:4, :]
    order = first + ((z + offset) & (RING - 1)) * share + which + seat_core * (RING * share)
    count, span = rows.shape
    columns = order.shape[1]
    planes = high.shape[0] // count
    pick = lax.broadcasted_iota(jnp.int32, (span, columns), 0) == order
    wide = jnp.dot(rows[...], pick.astype(jnp.float32), precision=lax.Precision.HIGHEST, preferred_element_type=jnp.float32)
    row = lax.broadcasted_iota(jnp.int32, (planes, columns), 0)
    col = lax.broadcasted_iota(jnp.int32, (planes, columns), 1)
    same = (col & (planes - 1)) == row
    for j in range(count):
        full = jnp.where(same, wide[j : j + 1, :], 0.0)
        top = full.astype(jnp.bfloat16).astype(jnp.float32)
        high[j * planes : (j + 1) * planes, :] = top
        low[j * planes : (j + 1) * planes, :] = full - top


def weights(rotation, plan, z, core, chip, share, planes):
    turned = rotation.T
    count = turned.shape[0]
    panel = CORES * RING * share
    per = LANES // panel
    table = np.repeat(np.asarray([(o, i, c, share) for o, i, c in plan], np.int32).T, planes, axis=1)
    table = np.concatenate([table, np.zeros((8 - table.shape[0], table.shape[1]), np.int32)])
    scalars = jnp.stack([z, core, (chip % per) * panel, chip // per])
    shape = (count * planes, table.shape[1])
    return pl.pallas_call(
        weights_body,
        grid_spec=pltpu.PrefetchScalarGridSpec(
            num_scalar_prefetch=1,
            grid=(1,),
            in_specs=[
                pl.BlockSpec((count, LANES), lambda i, s: (0, s[3])),
                pl.BlockSpec(table.shape, lambda i, s: (0, 0)),
            ],
            out_specs=[pl.BlockSpec(shape, lambda i, s: (0, 0))] * 2,
        ),
        out_shape=[jax.ShapeDtypeStruct(shape, jnp.float32)] * 2,
        compiler_params=room(6),
        cost_estimate=pl.CostEstimate(flops=10**6, bytes_accessed=10**6, transcendentals=0),
    )(scalars, turned, jnp.asarray(table))


def panel_body(acc, *rest):
    blocks, (high, low, out) = rest[:-3], rest[-3:]
    n, planes, width = acc.shape
    block = jnp.concatenate([b[...].reshape(b.shape[0] * planes, width) for b in blocks], axis=0)
    block_high = block.astype(jnp.bfloat16)
    block_low = (block - block_high.astype(jnp.float32)).astype(jnp.bfloat16)
    high = high[...].astype(jnp.bfloat16)
    low = low[...].astype(jnp.bfloat16)
    dot = lambda a, b: jnp.dot(a, b, preferred_element_type=jnp.float32)
    prod = dot(high, block_high) + (dot(high, block_low) + dot(low, block_high))
    out[...] = acc[...] + prod.reshape(n, planes, width)


def add_panel(acc, blocks, high, low):
    n, planes, cells = acc.shape
    chunk = cells // 4
    spec = lambda m: pl.BlockSpec((m, planes, chunk), lambda i: (0, 0, i))
    k = sum(b.shape[0] for b in blocks)
    full = pl.BlockSpec(high.shape, lambda i: (0, 0))
    return pl.pallas_call(
        panel_body,
        grid=(cells // chunk,),
        in_specs=[spec(n)] + [spec(b.shape[0]) for b in blocks] + [full, full],
        out_specs=spec(n),
        out_shape=jax.ShapeDtypeStruct(acc.shape, jnp.float32),
        compiler_params=room(20),
        cost_estimate=pl.CostEstimate(
            flops=6 * n * planes * planes * k * cells, bytes_accessed=4 * (2 * n + k) * planes * cells, transcendentals=0
        ),
    )(acc, *blocks, high, low)


def seat(x, z, core):
    return (x * RING + z % RING) * CORES + core


def everywhere(step):
    return [
        (seat(x, z, c), seat(*step(x, z, c))) for x in range(ROWS_X) for z in range(RING) for c in range(CORES)
    ]


ONWARD = everywhere(lambda x, z, c: (x, z + 1, c))
BACK = everywhere(lambda x, z, c: (x, z - 1, c))
ACROSS = everywhere(lambda x, z, c: (1 - x, z, c))
PARTNER = everywhere(lambda x, z, c: (x, z, 1 - c))


def pick_body(place, hand, moved, out):
    for m in range(out.shape[0]):
        out[m] = jnp.where(place[1] == 0, hand[m], moved[min(m, moved.shape[0] - 1)])


def pick(block, place, step, moved):
    n, planes, cells = block.shape
    share = n // RING
    hand = lambda index: pl.BlockSpec((share, planes, cells), index)
    return pl.pallas_call(
        pick_body,
        grid_spec=pltpu.PrefetchScalarGridSpec(
            num_scalar_prefetch=1,
            grid=(1,),
            in_specs=[
                hand(lambda i, s: ((s[0] + step) & (RING - 1), 0, 0)),
                pl.BlockSpec(memory_space=pltpu.VMEM),
            ],
            out_specs=pl.BlockSpec(memory_space=pltpu.VMEM),
        ),
        out_shape=jax.ShapeDtypeStruct((share, planes, cells), jnp.float32),
        compiler_params=room(3),
        cost_estimate=pl.CostEstimate(flops=0, bytes_accessed=12 * share * planes * cells, transcendentals=0),
    )(place, block, moved)


def settle_body(place, own, up, down, piece, *ends):
    offset = place[1]
    half = own.shape[0] // 2
    for m in range(own.shape[0]):
        middle = up[m] if m < half else down[m - half]
        far = jnp.where(offset < 4, up[m], jnp.where(offset == 4, middle, down[m]))
        piece[m] = jnp.where(offset == 0, own[m], far)
    if ends:
        pack_body(piece, *ends)


def settle(block, place, up, down, packed):
    share, planes, cells = up.shape
    hand = lambda index: pl.BlockSpec((share, planes, cells), index)
    still = pl.BlockSpec(memory_space=pltpu.VMEM)
    thin = (share, planes, cells * WIDTH // planes)
    shapes = [up.shape] + [thin] * (2 if packed else 0)
    return pl.pallas_call(
        settle_body,
        grid_spec=pltpu.PrefetchScalarGridSpec(
            num_scalar_prefetch=1,
            grid=(1,),
            in_specs=[hand(lambda i, s: (s[0], 0, 0)), still, still],
            out_specs=[still] * len(shapes),
        ),
        out_shape=[jax.ShapeDtypeStruct(shape, jnp.float32) for shape in shapes],
        compiler_params=room(5),
        cost_estimate=pl.CostEstimate(flops=0, bytes_accessed=20 * share * planes * cells, transcendentals=0),
    )(place, block, up, down)


def relay(block, place, packed):
    share = block.shape[0] // RING
    half = share // 2
    start = ((place[0] + 4) & (RING - 1)) * share
    size = (half,) + block.shape[1:]
    up = lax.ppermute(lax.dynamic_slice(block, (start, 0, 0), size), "band", ONWARD)
    down = lax.ppermute(lax.dynamic_slice(block, (start + half, 0, 0), size), "band", BACK)
    for step in (3, 2, 1):
        up = pick(block, place, step, up)
        down = pick(block, place, RING - step, down)
        up = lax.ppermute(up, "band", ONWARD)
        down = lax.ppermute(down, "band", BACK)
    return settle(block, place, up, down, packed)


def halo(head, tail):
    size = lax.axis_size("domain")
    low = lax.ppermute(tail, "domain", [(i, (i + 1) % size) for i in range(size)])
    high = lax.ppermute(head, "domain", [((i + 1) % size, i) for i in range(size)])
    return low, high


def step(orbitals, previous, potential, rotation, accumulated, panel):
    count = orbitals.shape[0]
    share = count // RING
    where = lax.axis_index("band")
    x, z, core = where >> 4, (where >> 1) & 7, where & 1
    chip = panel[0] & (ROWS_X * RING - 1)
    root_x, root_z = chip >> 3, chip & 7

    offset = (z - root_z) & (RING - 1)

    early = count // 2
    ends = pack(orbitals, 0, early)
    sides_early = halo(*ends)
    ends = pack(orbitals, early, count - early)
    sides_late = halo(*ends)

    place = jnp.stack([z, offset])
    piece, *ends = relay(orbitals, place, True)
    (before,) = relay(previous, place, False)
    below, above = halo(*ends)
    piece = apply_filter(piece, below, above, before, potential)
    other = lax.ppermute(piece, "band", ACROSS)
    piece = jnp.where(x == root_x, piece, other)
    filtered = apply_filter(orbitals, *sides_early, previous, potential)
    filtered = apply_filter(orbitals, *sides_late, previous, potential, early, filtered)

    blocks = [piece]
    plan = [(0, 0), (0, 1)]
    up = down = piece
    for hop in (1, 2, 3):
        up = lax.ppermute(up, "band", ONWARD)
        down = lax.ppermute(down, "band", BACK)
        blocks += [up, down]
        plan += [(-hop, 0), (-hop, 1), (hop, 0), (hop, 1)]
    blocks += [lax.ppermute(up, "band", ONWARD)]
    plan += [(-4, 0), (-4, 1)]
    blocks += [lax.ppermute(b, "band", PARTNER) for b in blocks]
    plan = [(o, i, c) for c in range(CORES) for o, i in plan]
    coefficients = weights(rotation, plan, z, core, chip, share, orbitals.shape[1])
    rotated = add_panel(accumulated, blocks, *coefficients)
    return filtered, rotated


def solution(mesh):
    in_specs = (
        P("band", "domain", None),
        P("band", "domain", None),
        P("domain", None),
        P(None, "band"),
        P("band", "domain", None),
        P(),
    )
    out_specs = (P("band", "domain", None), P("band", "domain", None))
    return jax.shard_map(step, mesh=mesh, in_specs=in_specs, out_specs=out_specs, check_vma=False)
```

```python
import math

import numpy as np
import jax
import jax.numpy as jnp
from jax import lax
from jax.experimental import pallas as pl
from jax.experimental.pallas import tpu as pltpu
from jax.sharding import PartitionSpec as P


coefs = (
    -5369.0 / 1800.0,
    12.0 / 7.0,
    -15.0 / 56.0,
    10.0 / 189.0,
    -1.0 / 112.0,
    2.0 / 1925.0,
    -1.0 / 16632.0,
)
SCALE = -2.0 / 14.0
ROW = 64
LANES = 128
WIDTH = 6
ROWS_X = 2
RING = 8
CORES = 2


def room(mib):
    return pltpu.CompilerParams(vmem_limit_bytes=mib << 20)


def row_matrix():
    out = np.zeros((LANES, LANES))
    for i in range(LANES):
        base = i - i % ROW
        for k in range(1, 7):
            for s in (k, -k):
                out[base + (i + s) % ROW, i] += SCALE * coefs[k]
    return out.astype(np.float32)


def mixed(full, spare, limit, below):
    sub = lax.broadcasted_iota(jnp.int32, full.shape, 0)
    return jnp.where(sub < limit, full, spare) if below else jnp.where(sub >= limit, full, spare)


def pack_body(orb, head, tail):
    for i in range(orb.shape[0]):
        for g in range(orb.shape[2] // (4 * LANES)):
            tiles = [orb[i, :, (4 * g + m) * LANES : (4 * g + m + 1) * LANES] for m in range(4)]
            for m in range(3):
                spare = pltpu.roll(tiles[3], 6 - 2 * m, 0)
                span = slice((3 * g + m) * LANES, (3 * g + m + 1) * LANES)
                head[i, :, span] = mixed(tiles[m], spare, WIDTH, True)
                tail[i, :, span] = mixed(tiles[m], spare, 2, False)


def unpacked(side, i, first):
    out = []
    for g in range(side.shape[2] // (3 * LANES)):
        three = [side[i, :, (3 * g + m) * LANES : (3 * g + m + 1) * LANES] for m in range(3)]
        rolled = [pltpu.roll(v, 2 + 2 * m, 0) for m, v in enumerate(three)]
        last = mixed(rolled[0], mixed(rolled[1], rolled[2], first + 4, True), first + 2, True)
        out += three + [last]
    return out


def pack(orb, first=0, n=None):
    n = n or orb.shape[0]
    planes, cells = orb.shape[1:]
    thin = cells * WIDTH // planes
    step = math.gcd(4, n, first)
    return pl.pallas_call(
        pack_body,
        grid=(n // step,),
        in_specs=[pl.BlockSpec((step, planes, cells), lambda i: (i + first // step, 0, 0))],
        out_specs=[pl.BlockSpec((step, planes, thin), lambda i: (i, 0, 0))] * 2,
        out_shape=[jax.ShapeDtypeStruct((n, planes, thin), jnp.float32)] * 2,
        compiler_params=room(8),
        cost_estimate=pl.CostEstimate(flops=0, bytes_accessed=10 * n * planes * cells, transcendentals=0),
    )(orb)


def filter_one(i, orb, low, high, prev, pot, mat, out, ext, half, rowsum):
    planes = orb.shape[1]
    tiles = orb.shape[2] // LANES
    span = 3 * planes
    low_tiles = unpacked(low, i, 2)
    high_tiles = unpacked(high, i, 0)
    lane = lax.broadcasted_iota(jnp.int32, (planes, LANES), 1)
    rolled = None
    first = None
    for t in range(tiles):
        tile = orb[i, :, t * LANES : (t + 1) * LANES]
        ext[span * t : span * t + planes, :] = low_tiles[t]
        ext[span * t + planes : span * t + 2 * planes, :] = tile
        ext[span * t + 2 * planes : span * t + 3 * planes, :] = high_tiles[t]
        now = pltpu.roll(tile, ROW, 1)
        if t:
            half[(t - 1) * planes : t * planes, :] = jnp.where(lane < ROW, rolled, now)
        else:
            first = now
        rolled = now
    half[(tiles - 1) * planes : tiles * planes, :] = jnp.where(lane < ROW, rolled, first)
    cells = jnp.concatenate([orb[i, :, t * LANES : (t + 1) * LANES] for t in range(tiles)], axis=0)
    rowsum[...] = jnp.dot(cells, mat[...], precision=lax.Precision.HIGHEST, preferred_element_type=jnp.float32)
    for t in range(tiles):
        base = span * t + planes
        centre = orb[i, :, t * LANES : (t + 1) * LANES]

        def flat(step):
            u = (t + step) % tiles
            return orb[i, :, u * LANES : (u + 1) * LANES]

        def odd(step):
            u = (t + step) % tiles
            return half[u * planes : (u + 1) * planes, :]

        total = rowsum[t * planes : (t + 1) * planes, :]
        for k in range(1, 7):
            pair = ext[base + k : base + k + planes, :] + ext[base - k : base - k + planes, :]
            if k % 2:
                pair = pair + (odd((k - 1) // 2) + odd(-(k + 1) // 2))
            else:
                pair = pair + (flat(k // 2) + flat(-(k // 2)))
            total = total + np.float32(SCALE * coefs[k]) * pair
        diag = pot[:, t * LANES : (t + 1) * LANES] * np.float32(1 / 14.0) + np.float32(3 * SCALE * coefs[0] - 36.0 / 14.0)
        out[i, :, t * LANES : (t + 1) * LANES] = total + diag * centre - prev[i, :, t * LANES : (t + 1) * LANES]


def filter_body(orb, low, high, prev, pot, mat, *rest):
    @pl.loop(0, orb.shape[0])
    def _(i):
        filter_one(i, orb, low, high, prev, pot, mat, *rest[-4:])


def apply_filter(orb, low, high, prev, pot, first=0, n=None, side=0, out=0, into=None, total=None):
    planes, cells = orb.shape[1:]
    n = n or low.shape[0]
    total = total or orb.shape[0]
    tiles = cells // LANES
    thin = cells * WIDTH // planes
    step = math.gcd(4, n, first, side, out)
    block = lambda start, width: pl.BlockSpec((step, planes, width), lambda i: (i + start // step, 0, 0))
    args = [orb, low, high, prev, pot, jnp.asarray(row_matrix())]
    specs = [
        block(first, cells),
        block(side, thin),
        block(side, thin),
        block(first, cells),
        pl.BlockSpec((planes, cells), lambda i: (0, 0)),
        pl.BlockSpec((LANES, LANES), lambda i: (0, 0)),
    ]
    if into is not None:
        args.append(into)
        specs.append(pl.BlockSpec(memory_space=pl.ANY))
    return pl.pallas_call(
        filter_body,
        grid=(n // step,),
        in_specs=specs,
        out_specs=block(out, cells),
        out_shape=jax.ShapeDtypeStruct((total, planes, cells), jnp.float32),
        input_output_aliases={} if into is None else {6: 0},
        scratch_shapes=[
            pltpu.VMEM((tiles * 3 * planes, LANES), jnp.float32),
            pltpu.VMEM((tiles * planes, LANES), jnp.float32),
            pltpu.VMEM((tiles * planes, LANES), jnp.float32),
        ],
        compiler_params=room(14),
        cost_estimate=pl.CostEstimate(
            flops=n * planes * cells * 1600, bytes_accessed=19 * n * planes * cells, transcendentals=0
        ),
    )(*args)


def weights_body(scalars, rows, plan, high, low):
    z, core, first = scalars[0], scalars[1], scalars[2]
    offset, which, other = plan[0:1, :], plan[1:2, :], plan[2:3, :]
    seat_core = jnp.where(other == 1, 1 - core, core)
    share = plan[3:4, :]
    order = first + ((z + offset) & (RING - 1)) * share + which + seat_core * (RING * share)
    count, span = rows.shape
    columns = order.shape[1]
    planes = high.shape[0] // count
    pick = lax.broadcasted_iota(jnp.int32, (span, columns), 0) == order
    wide = jnp.dot(rows[...], pick.astype(jnp.float32), precision=lax.Precision.HIGHEST, preferred_element_type=jnp.float32)
    row = lax.broadcasted_iota(jnp.int32, (planes, columns), 0)
    col = lax.broadcasted_iota(jnp.int32, (planes, columns), 1)
    same = (col & (planes - 1)) == row
    for j in range(count):
        full = jnp.where(same, wide[j : j + 1, :], 0.0)
        top = full.astype(jnp.bfloat16).astype(jnp.float32)
        high[j * planes : (j + 1) * planes, :] = top
        low[j * planes : (j + 1) * planes, :] = full - top


def weights(rotation, plan, z, core, chip, share, planes):
    turned = rotation.T
    count = turned.shape[0]
    panel = CORES * RING * share
    per = LANES // panel
    table = np.repeat(np.asarray([(o, i, c, share) for o, i, c in plan], np.int32).T, planes, axis=1)
    table = np.concatenate([table, np.zeros((8 - table.shape[0], table.shape[1]), np.int32)])
    scalars = jnp.stack([z, core, (chip % per) * panel, chip // per])
    shape = (count * planes, table.shape[1])
    return pl.pallas_call(
        weights_body,
        grid_spec=pltpu.PrefetchScalarGridSpec(
            num_scalar_prefetch=1,
            grid=(1,),
            in_specs=[
                pl.BlockSpec((count, LANES), lambda i, s: (0, s[3])),
                pl.BlockSpec(table.shape, lambda i, s: (0, 0)),
            ],
            out_specs=[pl.BlockSpec(shape, lambda i, s: (0, 0))] * 2,
        ),
        out_shape=[jax.ShapeDtypeStruct(shape, jnp.float32)] * 2,
        compiler_params=room(6),
        cost_estimate=pl.CostEstimate(flops=10**6, bytes_accessed=10**6, transcendentals=0),
    )(scalars, turned, jnp.asarray(table))


def panel_body(acc, *rest):
    blocks, (high, low, out) = rest[:-3], rest[-3:]
    n, planes, width = acc.shape
    block = jnp.concatenate([b[...].reshape(b.shape[0] * planes, width) for b in blocks], axis=0)
    block_high = block.astype(jnp.bfloat16)
    block_low = (block - block_high.astype(jnp.float32)).astype(jnp.bfloat16)
    high = high[...].astype(jnp.bfloat16)
    low = low[...].astype(jnp.bfloat16)
    dot = lambda a, b: jnp.dot(a, b, preferred_element_type=jnp.float32)
    prod = dot(high, block_high) + (dot(high, block_low) + dot(low, block_high))
    out[...] = acc[...] + prod.reshape(n, planes, width)


def add_panel(acc, blocks, high, low):
    n, planes, cells = acc.shape
    chunk = cells // 4
    spec = lambda m: pl.BlockSpec((m, planes, chunk), lambda i: (0, 0, i))
    k = sum(b.shape[0] for b in blocks)
    full = pl.BlockSpec(high.shape, lambda i: (0, 0))
    return pl.pallas_call(
        panel_body,
        grid=(cells // chunk,),
        in_specs=[spec(n)] + [spec(b.shape[0]) for b in blocks] + [full, full],
        out_specs=spec(n),
        out_shape=jax.ShapeDtypeStruct(acc.shape, jnp.float32),
        compiler_params=room(20),
        cost_estimate=pl.CostEstimate(
            flops=6 * n * planes * planes * k * cells, bytes_accessed=4 * (2 * n + k) * planes * cells, transcendentals=0
        ),
    )(acc, *blocks, high, low)


def seat(x, z, core):
    return (x * RING + z % RING) * CORES + core


def everywhere(step):
    return [
        (seat(x, z, c), seat(*step(x, z, c))) for x in range(ROWS_X) for z in range(RING) for c in range(CORES)
    ]


ONWARD = everywhere(lambda x, z, c: (x, z + 1, c))
BACK = everywhere(lambda x, z, c: (x, z - 1, c))
ACROSS = everywhere(lambda x, z, c: (1 - x, z, c))
PARTNER = everywhere(lambda x, z, c: (x, z, 1 - c))


def pick_body(place, hand, moved, out):
    for m in range(out.shape[0]):
        out[m] = jnp.where(place[1] == 0, hand[m], moved[min(m, moved.shape[0] - 1)])


def pick(block, place, step, moved):
    n, planes, cells = block.shape
    share = n // RING
    hand = lambda index: pl.BlockSpec((share, planes, cells), index)
    return pl.pallas_call(
        pick_body,
        grid_spec=pltpu.PrefetchScalarGridSpec(
            num_scalar_prefetch=1,
            grid=(1,),
            in_specs=[
                hand(lambda i, s: ((s[0] + step) & (RING - 1), 0, 0)),
                pl.BlockSpec(memory_space=pltpu.VMEM),
            ],
            out_specs=pl.BlockSpec(memory_space=pltpu.VMEM),
        ),
        out_shape=jax.ShapeDtypeStruct((share, planes, cells), jnp.float32),
        compiler_params=room(3),
        cost_estimate=pl.CostEstimate(flops=0, bytes_accessed=12 * share * planes * cells, transcendentals=0),
    )(place, block, moved)


def settle_body(place, own, up, down, piece, *ends):
    offset = place[1]
    half = own.shape[0] // 2
    for m in range(own.shape[0]):
        middle = up[m] if m < half else down[m - half]
        far = jnp.where(offset < 4, up[m], jnp.where(offset == 4, middle, down[m]))
        piece[m] = jnp.where(offset == 0, own[m], far)
    if ends:
        pack_body(piece, *ends)


def settle(block, place, up, down, packed):
    share, planes, cells = up.shape
    hand = lambda index: pl.BlockSpec((share, planes, cells), index)
    still = pl.BlockSpec(memory_space=pltpu.VMEM)
    thin = (share, planes, cells * WIDTH // planes)
    shapes = [up.shape] + [thin] * (2 if packed else 0)
    return pl.pallas_call(
        settle_body,
        grid_spec=pltpu.PrefetchScalarGridSpec(
            num_scalar_prefetch=1,
            grid=(1,),
            in_specs=[hand(lambda i, s: (s[0], 0, 0)), still, still],
            out_specs=[still] * len(shapes),
        ),
        out_shape=[jax.ShapeDtypeStruct(shape, jnp.float32) for shape in shapes],
        compiler_params=room(5),
        cost_estimate=pl.CostEstimate(flops=0, bytes_accessed=20 * share * planes * cells, transcendentals=0),
    )(place, block, up, down)


def keep_body(flag, mine, other, out):
    out[...] = jnp.where(flag[0] == 1, mine[...], other[...])


def keep(flag, mine, other):
    whole = pl.BlockSpec(memory_space=pltpu.VMEM)
    return pl.pallas_call(
        keep_body,
        in_specs=[pl.BlockSpec(memory_space=pltpu.SMEM), whole, whole],
        out_specs=whole,
        out_shape=jax.ShapeDtypeStruct(mine.shape, jnp.float32),
        compiler_params=room(2),
        cost_estimate=pl.CostEstimate(flops=0, bytes_accessed=12 * mine.size, transcendentals=0),
    )(flag, mine, other)


def stack_body(*refs):
    out = refs[-1]
    for i, ref in enumerate(refs[:-1]):
        out[i] = ref[0]


def stacked(blocks):
    whole = pl.BlockSpec(memory_space=pltpu.VMEM)
    shape = (len(blocks),) + blocks[0].shape[1:]
    return pl.pallas_call(
        stack_body,
        in_specs=[whole] * len(blocks),
        out_specs=whole,
        out_shape=jax.ShapeDtypeStruct(shape, jnp.float32),
        compiler_params=room(3),
        cost_estimate=pl.CostEstimate(flops=0, bytes_accessed=8 * math.prod(shape), transcendentals=0),
    )(*blocks)


def relay(block, place, packed):
    share = block.shape[0] // RING
    half = share // 2
    start = ((place[0] + 4) & (RING - 1)) * share
    size = (half,) + block.shape[1:]
    up = lax.ppermute(lax.dynamic_slice(block, (start, 0, 0), size), "band", ONWARD)
    down = lax.ppermute(lax.dynamic_slice(block, (start + half, 0, 0), size), "band", BACK)
    for step in (3, 2, 1):
        up = pick(block, place, step, up)
        down = pick(block, place, RING - step, down)
        up = lax.ppermute(up, "band", ONWARD)
        down = lax.ppermute(down, "band", BACK)
    return settle(block, place, up, down, packed)


def halo(head, tail):
    size = lax.axis_size("domain")
    low = lax.ppermute(tail, "domain", [(i, (i + 1) % size) for i in range(size)])
    high = lax.ppermute(head, "domain", [((i + 1) % size, i) for i in range(size)])
    return low, high


def step(orbitals, previous, potential, rotation, accumulated, panel):
    count = orbitals.shape[0]
    share = count // RING
    where = lax.axis_index("band")
    x, z, core = where >> 4, (where >> 1) & 7, where & 1
    chip = panel[0] & (ROWS_X * RING - 1)
    root_x, root_z = chip >> 3, chip & 7

    offset = (z - root_z) & (RING - 1)

    early = count * 5 // 8
    ends = pack(orbitals, 0, early)
    sides_early = halo(*ends)
    ends = pack(orbitals, early, count - early)
    sides_late = halo(*ends)

    place = jnp.stack([z, offset])
    piece, *ends = relay(orbitals, place, True)
    (before,) = relay(previous, place, False)
    below, above = halo(*ends)
    filtered = apply_filter(orbitals, *sides_early, previous, potential)
    filtered = apply_filter(orbitals, *sides_late, previous, potential, early, out=early, into=filtered)

    flag = (x == root_x).astype(jnp.int32)[None]
    chains = []
    for m in range(share):
        mine = apply_filter(piece, below, above, before, potential, m, 1, m, total=1)
        other = lax.ppermute(mine, "band", ACROSS)
        chains.append([keep(flag, mine, other)] * 2)
    rounds = [[(chain[0], 0, m) for m, chain in enumerate(chains)]]
    for hop in range(1, RING // 2 + 1):
        rounds.append([])
        for m, chain in enumerate(chains):
            for way, pairs in enumerate((ONWARD, BACK)):
                if hop == RING // 2 and way != m % 2:
                    continue
                chain[way] = lax.ppermute(chain[way], "band", pairs)
                rounds[-1].append((chain[way], hop if way else -hop, m))
    rounds[:2] = [rounds[0] + rounds[1]]
    mine, theirs, plan = [], [], []
    for arrived in rounds:
        mine += [block for block, _, _ in arrived]
        plan += [(off, m) for _, off, m in arrived]
        group = stacked([block for block, _, _ in arrived])
        theirs.append(lax.ppermute(group, "band", PARTNER))
    blocks = mine + theirs
    plan = [(o, i, c) for c in range(CORES) for o, i in plan]
    coefficients = weights(rotation, plan, z, core, chip, share, orbitals.shape[1])
    rotated = add_panel(accumulated, blocks, *coefficients)
    return filtered, rotated


def solution(mesh):
    in_specs = (
        P("band", "domain", None),
        P("band", "domain", None),
        P("domain", None),
        P(None, "band"),
        P("band", "domain", None),
        P(),
    )
    out_specs = (P("band", "domain", None), P("band", "domain", None))
    return jax.shard_map(step, mesh=mesh, in_specs=in_specs, out_specs=out_specs, check_vma=False)
```

```python
import math

import numpy as np
import jax
import jax.numpy as jnp
from jax import lax
from jax.experimental import pallas as pl
from jax.experimental.pallas import tpu as pltpu
from jax.sharding import PartitionSpec as P


coefs = (
    -5369.0 / 1800.0,
    12.0 / 7.0,
    -15.0 / 56.0,
    10.0 / 189.0,
    -1.0 / 112.0,
    2.0 / 1925.0,
    -1.0 / 16632.0,
)
SCALE = -2.0 / 14.0
ROW = 64
LANES = 128
WIDTH = 6
ROWS_X = 2
RING = 8
CORES = 2


def split(*counts):
    return max(d for d in range(1, 6) if math.gcd(*counts) % d == 0)


def room(mib):
    return pltpu.CompilerParams(vmem_limit_bytes=mib << 20)


def row_matrix():
    out = np.zeros((LANES, LANES))
    for i in range(LANES):
        base = i - i % ROW
        for k in range(1, 7):
            for s in (k, -k):
                out[base + (i + s) % ROW, i] += SCALE * coefs[k]
    return out.astype(np.float32)


def mixed(full, spare, limit, below):
    sub = lax.broadcasted_iota(jnp.int32, full.shape, 0)
    return jnp.where(sub < limit, full, spare) if below else jnp.where(sub >= limit, full, spare)


def pack_body(orb, head, tail):
    for i in range(orb.shape[0]):
        for g in range(orb.shape[2] // (4 * LANES)):
            tiles = [orb[i, :, (4 * g + m) * LANES : (4 * g + m + 1) * LANES] for m in range(4)]
            for m in range(3):
                spare = pltpu.roll(tiles[3], 6 - 2 * m, 0)
                span = slice((3 * g + m) * LANES, (3 * g + m + 1) * LANES)
                head[i, :, span] = mixed(tiles[m], spare, WIDTH, True)
                tail[i, :, span] = mixed(tiles[m], spare, 2, False)


def unpacked(side, i, first):
    out = []
    for g in range(side.shape[2] // (3 * LANES)):
        three = [side[i, :, (3 * g + m) * LANES : (3 * g + m + 1) * LANES] for m in range(3)]
        rolled = [pltpu.roll(v, 2 + 2 * m, 0) for m, v in enumerate(three)]
        last = mixed(rolled[0], mixed(rolled[1], rolled[2], first + 4, True), first + 2, True)
        out += three + [last]
    return out


def pack(orb, first=0, n=None):
    n = n or orb.shape[0]
    planes, cells = orb.shape[1:]
    thin = cells * WIDTH // planes
    step = split(n, first)
    return pl.pallas_call(
        pack_body,
        grid=(n // step,),
        in_specs=[pl.BlockSpec((step, planes, cells), lambda i: (i + first // step, 0, 0))],
        out_specs=[pl.BlockSpec((step, planes, thin), lambda i: (i, 0, 0))] * 2,
        out_shape=[jax.ShapeDtypeStruct((n, planes, thin), jnp.float32)] * 2,
        compiler_params=room(8),
        cost_estimate=pl.CostEstimate(flops=0, bytes_accessed=10 * n * planes * cells, transcendentals=0),
    )(orb)


def halves(values):
    high = values.astype(jnp.bfloat16)
    return high, (values - high.astype(jnp.float32)).astype(jnp.bfloat16)


def three_pass(left, right):
    left_high, left_low = halves(left)
    right_high, right_low = halves(right)
    dot = lambda a, b: jnp.dot(a, b, preferred_element_type=jnp.float32)
    return dot(left_high, right_high) + (dot(left_high, right_low) + dot(left_low, right_high))


def filter_one(i, orb, low, high, prev, pot, mat, out, ext, half, rowsum):
    planes = orb.shape[1]
    tiles = orb.shape[2] // LANES
    span = 3 * planes
    low_tiles = unpacked(low, i, 2)
    high_tiles = unpacked(high, i, 0)
    lane = lax.broadcasted_iota(jnp.int32, (planes, LANES), 1)
    rolled = None
    first = None
    for t in range(tiles):
        tile = orb[i, :, t * LANES : (t + 1) * LANES]
        ext[span * t : span * t + planes, :] = low_tiles[t]
        ext[span * t + planes : span * t + 2 * planes, :] = tile
        ext[span * t + 2 * planes : span * t + 3 * planes, :] = high_tiles[t]
        now = pltpu.roll(tile, ROW, 1)
        if t:
            half[(t - 1) * planes : t * planes, :] = jnp.where(lane < ROW, rolled, now)
        else:
            first = now
        rolled = now
    half[(tiles - 1) * planes : tiles * planes, :] = jnp.where(lane < ROW, rolled, first)
    cells = jnp.concatenate([orb[i, :, t * LANES : (t + 1) * LANES] for t in range(tiles)], axis=0)
    rowsum[...] = three_pass(cells, mat[...])
    for t in range(tiles):
        base = span * t + planes
        centre = orb[i, :, t * LANES : (t + 1) * LANES]

        def flat(step):
            u = (t + step) % tiles
            return orb[i, :, u * LANES : (u + 1) * LANES]

        def odd(step):
            u = (t + step) % tiles
            return half[u * planes : (u + 1) * planes, :]

        total = rowsum[t * planes : (t + 1) * planes, :]
        for k in range(1, 7):
            pair = ext[base + k : base + k + planes, :] + ext[base - k : base - k + planes, :]
            if k % 2:
                pair = pair + (odd((k - 1) // 2) + odd(-(k + 1) // 2))
            else:
                pair = pair + (flat(k // 2) + flat(-(k // 2)))
            total = total + np.float32(SCALE * coefs[k]) * pair
        diag = pot[:, t * LANES : (t + 1) * LANES] * np.float32(1 / 14.0) + np.float32(3 * SCALE * coefs[0] - 36.0 / 14.0)
        out[i, :, t * LANES : (t + 1) * LANES] = total + diag * centre - prev[i, :, t * LANES : (t + 1) * LANES]


def filter_body(orb, low, high, prev, pot, mat, *rest):
    @pl.loop(0, orb.shape[0])
    def _(i):
        filter_one(i, orb, low, high, prev, pot, mat, *rest[-4:])


def apply_filter(orb, low, high, prev, pot, first=0, n=None, side=0, out=0, into=None, total=None):
    planes, cells = orb.shape[1:]
    n = n or low.shape[0]
    total = total or orb.shape[0]
    tiles = cells // LANES
    thin = cells * WIDTH // planes
    step = split(n, first, side, out)
    block = lambda start, width: pl.BlockSpec((step, planes, width), lambda i: (i + start // step, 0, 0))
    args = [orb, low, high, prev, pot, jnp.asarray(row_matrix())]
    specs = [
        block(first, cells),
        block(side, thin),
        block(side, thin),
        block(first, cells),
        pl.BlockSpec((planes, cells), lambda i: (0, 0)),
        pl.BlockSpec((LANES, LANES), lambda i: (0, 0)),
    ]
    if into is not None:
        args.append(into)
        specs.append(pl.BlockSpec(memory_space=pl.ANY))
    return pl.pallas_call(
        filter_body,
        grid=(n // step,),
        in_specs=specs,
        out_specs=block(out, cells),
        out_shape=jax.ShapeDtypeStruct((total, planes, cells), jnp.float32),
        input_output_aliases={} if into is None else {6: 0},
        scratch_shapes=[
            pltpu.VMEM((tiles * 3 * planes, LANES), jnp.float32),
            pltpu.VMEM((tiles * planes, LANES), jnp.float32),
            pltpu.VMEM((tiles * planes, LANES), jnp.float32),
        ],
        compiler_params=room(14),
        cost_estimate=pl.CostEstimate(
            flops=n * planes * cells * 1600, bytes_accessed=19 * n * planes * cells, transcendentals=0
        ),
    )(*args)


def weights_body(scalars, rows, plan, high, low):
    z, core, first = scalars[0], scalars[1], scalars[2]
    offset, which, other = plan[0:1, :], plan[1:2, :], plan[2:3, :]
    seat_core = jnp.where(other == 1, 1 - core, core)
    share = plan[3:4, :]
    order = first + ((z + offset) & (RING - 1)) * share + which + seat_core * (RING * share)
    count, span = rows.shape
    columns = order.shape[1]
    planes = high.shape[0] // count
    pick = lax.broadcasted_iota(jnp.int32, (span, columns), 0) == order
    wide = jnp.dot(rows[...], pick.astype(jnp.float32), precision=lax.Precision.HIGHEST, preferred_element_type=jnp.float32)
    row = lax.broadcasted_iota(jnp.int32, (planes, columns), 0)
    col = lax.broadcasted_iota(jnp.int32, (planes, columns), 1)
    same = (col & (planes - 1)) == row
    for j in range(count):
        full = jnp.where(same, wide[j : j + 1, :], 0.0)
        top = full.astype(jnp.bfloat16).astype(jnp.float32)
        high[j * planes : (j + 1) * planes, :] = top
        low[j * planes : (j + 1) * planes, :] = full - top


def weights(rotation, plan, z, core, chip, share, planes):
    turned = rotation.T
    count = turned.shape[0]
    panel = CORES * RING * share
    per = LANES // panel
    table = np.repeat(np.asarray([(o, i, c, share) for o, i, c in plan], np.int32).T, planes, axis=1)
    table = np.concatenate([table, np.zeros((8 - table.shape[0], table.shape[1]), np.int32)])
    scalars = jnp.stack([z, core, (chip % per) * panel, chip // per])
    shape = (count * planes, table.shape[1])
    return pl.pallas_call(
        weights_body,
        grid_spec=pltpu.PrefetchScalarGridSpec(
            num_scalar_prefetch=1,
            grid=(1,),
            in_specs=[
                pl.BlockSpec((count, LANES), lambda i, s: (0, s[3])),
                pl.BlockSpec(table.shape, lambda i, s: (0, 0)),
            ],
            out_specs=[pl.BlockSpec(shape, lambda i, s: (0, 0))] * 2,
        ),
        out_shape=[jax.ShapeDtypeStruct(shape, jnp.float32)] * 2,
        compiler_params=room(6),
        cost_estimate=pl.CostEstimate(flops=10**6, bytes_accessed=10**6, transcendentals=0),
    )(scalars, turned, jnp.asarray(table))


def panel_body(acc, *rest):
    blocks, (high, low, out) = rest[:-3], rest[-3:]
    n, planes, width = acc.shape
    block = jnp.concatenate([b[...].reshape(b.shape[0] * planes, width) for b in blocks], axis=0)
    block_high = block.astype(jnp.bfloat16)
    block_low = (block - block_high.astype(jnp.float32)).astype(jnp.bfloat16)
    high = high[...].astype(jnp.bfloat16)
    low = low[...].astype(jnp.bfloat16)
    dot = lambda a, b: jnp.dot(a, b, preferred_element_type=jnp.float32)
    prod = dot(high, block_high) + (dot(high, block_low) + dot(low, block_high))
    out[...] = acc[...] + prod.reshape(n, planes, width)


def add_panel(acc, blocks, high, low):
    n, planes, cells = acc.shape
    chunk = cells // 4
    spec = lambda m: pl.BlockSpec((m, planes, chunk), lambda i: (0, 0, i))
    k = sum(b.shape[0] for b in blocks)
    full = pl.BlockSpec(high.shape, lambda i: (0, 0))
    return pl.pallas_call(
        panel_body,
        grid=(cells // chunk,),
        in_specs=[spec(n)] + [spec(b.shape[0]) for b in blocks] + [full, full],
        out_specs=spec(n),
        out_shape=jax.ShapeDtypeStruct(acc.shape, jnp.float32),
        compiler_params=room(20),
        cost_estimate=pl.CostEstimate(
            flops=6 * n * planes * planes * k * cells, bytes_accessed=4 * (2 * n + k) * planes * cells, transcendentals=0
        ),
    )(acc, *blocks, high, low)


def seat(x, z, core):
    return (x * RING + z % RING) * CORES + core


def everywhere(step):
    return [
        (seat(x, z, c), seat(*step(x, z, c))) for x in range(ROWS_X) for z in range(RING) for c in range(CORES)
    ]


ONWARD = everywhere(lambda x, z, c: (x, z + 1, c))
BACK = everywhere(lambda x, z, c: (x, z - 1, c))
ACROSS = everywhere(lambda x, z, c: (1 - x, z, c))
PARTNER = everywhere(lambda x, z, c: (x, z, 1 - c))


def pick_body(place, hand_up, hand_down, up, down, out_up, out_down):
    for hand, moved, out in ((hand_up, up, out_up), (hand_down, down, out_down)):
        for m in range(out.shape[0]):
            out[m] = jnp.where(place[1] == 0, hand[m], moved[min(m, moved.shape[0] - 1)])


def pick(block, place, step, up, down):
    n, planes, cells = block.shape
    share = n // RING
    hand = lambda step: pl.BlockSpec((share, planes, cells), lambda i, s: ((s[0] + step) & (RING - 1), 0, 0))
    still = pl.BlockSpec(memory_space=pltpu.VMEM)
    return pl.pallas_call(
        pick_body,
        grid_spec=pltpu.PrefetchScalarGridSpec(
            num_scalar_prefetch=1,
            grid=(1,),
            in_specs=[hand(step), hand(RING - step), still, still],
            out_specs=[still, still],
        ),
        out_shape=[jax.ShapeDtypeStruct((share, planes, cells), jnp.float32)] * 2,
        compiler_params=room(5),
        cost_estimate=pl.CostEstimate(flops=0, bytes_accessed=24 * share * planes * cells, transcendentals=0),
    )(place, block, block, up, down)


def settle_body(place, own, up, down, piece, *ends):
    offset = place[1]
    half = own.shape[0] // 2
    for m in range(own.shape[0]):
        middle = up[m] if m < half else down[m - half]
        far = jnp.where(offset < 4, up[m], jnp.where(offset == 4, middle, down[m]))
        piece[m] = jnp.where(offset == 0, own[m], far)
    if ends:
        pack_body(piece, *ends)


def settle(block, place, up, down, packed):
    share, planes, cells = up.shape
    hand = lambda index: pl.BlockSpec((share, planes, cells), index)
    still = pl.BlockSpec(memory_space=pltpu.VMEM)
    thin = (share, planes, cells * WIDTH // planes)
    shapes = [up.shape] + [thin] * (2 if packed else 0)
    return pl.pallas_call(
        settle_body,
        grid_spec=pltpu.PrefetchScalarGridSpec(
            num_scalar_prefetch=1,
            grid=(1,),
            in_specs=[hand(lambda i, s: (s[0], 0, 0)), still, still],
            out_specs=[still] * len(shapes),
        ),
        out_shape=[jax.ShapeDtypeStruct(shape, jnp.float32) for shape in shapes],
        compiler_params=room(5),
        cost_estimate=pl.CostEstimate(flops=0, bytes_accessed=20 * share * planes * cells, transcendentals=0),
    )(place, block, up, down)


def keep_body(flag, mine, other, out):
    out[...] = jnp.where(flag[0] == 1, mine[...], other[...])


def keep(flag, mine, other):
    whole = pl.BlockSpec(memory_space=pltpu.VMEM)
    return pl.pallas_call(
        keep_body,
        in_specs=[pl.BlockSpec(memory_space=pltpu.SMEM), whole, whole],
        out_specs=whole,
        out_shape=jax.ShapeDtypeStruct(mine.shape, jnp.float32),
        compiler_params=room(2),
        cost_estimate=pl.CostEstimate(flops=0, bytes_accessed=12 * mine.size, transcendentals=0),
    )(flag, mine, other)


def stack_body(*refs):
    out = refs[-1]
    for i, ref in enumerate(refs[:-1]):
        out[i] = ref[0]


def stacked(blocks):
    whole = pl.BlockSpec(memory_space=pltpu.VMEM)
    shape = (len(blocks),) + blocks[0].shape[1:]
    return pl.pallas_call(
        stack_body,
        in_specs=[whole] * len(blocks),
        out_specs=whole,
        out_shape=jax.ShapeDtypeStruct(shape, jnp.float32),
        compiler_params=room(3),
        cost_estimate=pl.CostEstimate(flops=0, bytes_accessed=8 * math.prod(shape), transcendentals=0),
    )(*blocks)


def relay(block, place, packed):
    share = block.shape[0] // RING
    half = share // 2
    start = ((place[0] + 4) & (RING - 1)) * share
    size = (half,) + block.shape[1:]
    up = lax.ppermute(lax.dynamic_slice(block, (start, 0, 0), size), "band", ONWARD)
    down = lax.ppermute(lax.dynamic_slice(block, (start + half, 0, 0), size), "band", BACK)
    for step in (3, 2, 1):
        up, down = pick(block, place, step, up, down)
        up = lax.ppermute(up, "band", ONWARD)
        down = lax.ppermute(down, "band", BACK)
    return settle(block, place, up, down, packed)


def halo(head, tail):
    size = lax.axis_size("domain")
    low = lax.ppermute(tail, "domain", [(i, (i + 1) % size) for i in range(size)])
    high = lax.ppermute(head, "domain", [((i + 1) % size, i) for i in range(size)])
    return low, high


def step(orbitals, previous, potential, rotation, accumulated, panel):
    count = orbitals.shape[0]
    share = count // RING
    where = lax.axis_index("band")
    x, z, core = where >> 4, (where >> 1) & 7, where & 1
    chip = panel[0] & (ROWS_X * RING - 1)
    root_x, root_z = chip >> 3, chip & 7

    offset = (z - root_z) & (RING - 1)

    early = count * 5 // 8
    ends = pack(orbitals, 0, early)
    sides_early = halo(*ends)
    ends = pack(orbitals, early, count - early)
    sides_late = halo(*ends)

    place = jnp.stack([z, offset])
    piece, *ends = relay(orbitals, place, True)
    (before,) = relay(previous, place, False)
    below, above = halo(*ends)
    filtered = apply_filter(orbitals, *sides_early, previous, potential)
    filtered = apply_filter(orbitals, *sides_late, previous, potential, early, out=early, into=filtered)

    flag = (x == root_x).astype(jnp.int32)[None]
    chains = []
    for m in range(share):
        mine = apply_filter(piece, below, above, before, potential, m, 1, m, total=1)
        other = lax.ppermute(mine, "band", ACROSS)
        chains.append([keep(flag, mine, other)] * 2)
    rounds = [[(chain[0], 0, m) for m, chain in enumerate(chains)]]
    for hop in range(1, RING // 2 + 1):
        rounds.append([])
        for m, chain in enumerate(chains):
            for way, pairs in enumerate((ONWARD, BACK)):
                if hop == RING // 2 and way != m % 2:
                    continue
                chain[way] = lax.ppermute(chain[way], "band", pairs)
                rounds[-1].append((chain[way], hop if way else -hop, m))
    rounds[:2] = [rounds[0] + rounds[1]]
    mine, theirs, plan = [], [], []
    for arrived in rounds:
        mine += [block for block, _, _ in arrived]
        plan += [(off, m) for _, off, m in arrived]
        group = stacked([block for block, _, _ in arrived])
        theirs.append(lax.ppermute(group, "band", PARTNER))
    blocks = mine + theirs
    plan = [(o, i, c) for c in range(CORES) for o, i in plan]
    coefficients = weights(rotation, plan, z, core, chip, share, orbitals.shape[1])
    rotated = add_panel(accumulated, blocks, *coefficients)
    return filtered, rotated


def solution(mesh):
    in_specs = (
        P("band", "domain", None),
        P("band", "domain", None),
        P("domain", None),
        P(None, "band"),
        P("band", "domain", None),
        P(),
    )
    out_specs = (P("band", "domain", None), P("band", "domain", None))
    return jax.shard_map(step, mesh=mesh, in_specs=in_specs, out_specs=out_specs, check_vma=False)
```

```python
import math

import numpy as np
import jax
import jax.numpy as jnp
from jax import lax
from jax.experimental import pallas as pl
from jax.experimental.pallas import tpu as pltpu
from jax.sharding import PartitionSpec as P


coefs = (
    -5369.0 / 1800.0,
    12.0 / 7.0,
    -15.0 / 56.0,
    10.0 / 189.0,
    -1.0 / 112.0,
    2.0 / 1925.0,
    -1.0 / 16632.0,
)
SCALE = -2.0 / 14.0
ROW = 64
LANES = 128
WIDTH = 6
ROWS_X = 2
RING = 8
CORES = 2


def split(*counts):
    return max(d for d in range(1, 6) if math.gcd(*counts) % d == 0)


def room(mib):
    return pltpu.CompilerParams(vmem_limit_bytes=mib << 20)


def row_matrix():
    out = np.zeros((LANES, LANES))
    for i in range(LANES):
        base = i - i % ROW
        for k in range(1, 7):
            for s in (k, -k):
                out[base + (i + s) % ROW, i] += SCALE * coefs[k]
    return out.astype(np.float32)


def mixed(full, spare, limit, below):
    sub = lax.broadcasted_iota(jnp.int32, full.shape, 0)
    return jnp.where(sub < limit, full, spare) if below else jnp.where(sub >= limit, full, spare)


def pack_one(i, orb, head, tail):
    for g in range(orb.shape[2] // (4 * LANES)):
        tiles = [orb[i, :, (4 * g + m) * LANES : (4 * g + m + 1) * LANES] for m in range(4)]
        for m in range(3):
            spare = pltpu.roll(tiles[3], 6 - 2 * m, 0)
            span = slice((3 * g + m) * LANES, (3 * g + m + 1) * LANES)
            head[i, :, span] = mixed(tiles[m], spare, WIDTH, True)
            tail[i, :, span] = mixed(tiles[m], spare, 2, False)


def pack_body(orb, head, tail):
    @pl.loop(0, head.shape[0])
    def _(i):
        pack_one(i, orb, head, tail)


def unpacked(side, i, first):
    out = []
    for g in range(side.shape[2] // (3 * LANES)):
        three = [side[i, :, (3 * g + m) * LANES : (3 * g + m + 1) * LANES] for m in range(3)]
        rolled = [pltpu.roll(v, 2 + 2 * m, 0) for m, v in enumerate(three)]
        last = mixed(rolled[0], mixed(rolled[1], rolled[2], first + 4, True), first + 2, True)
        out += three + [last]
    return out


def pack(orb, first=0, n=None):
    n = n or orb.shape[0]
    planes, cells = orb.shape[1:]
    thin = cells * WIDTH // planes
    step = split(n, first)
    return pl.pallas_call(
        pack_body,
        grid=(n // step,),
        in_specs=[pl.BlockSpec((step, planes, cells), lambda i: (i + first // step, 0, 0))],
        out_specs=[pl.BlockSpec((step, planes, thin), lambda i: (i, 0, 0))] * 2,
        out_shape=[jax.ShapeDtypeStruct((n, planes, thin), jnp.float32)] * 2,
        compiler_params=room(8),
        cost_estimate=pl.CostEstimate(flops=0, bytes_accessed=10 * n * planes * cells, transcendentals=0),
    )(orb)


def halves(values):
    high = values.astype(jnp.bfloat16)
    return high, (values - high.astype(jnp.float32)).astype(jnp.bfloat16)


def three_pass(left, right):
    left_high, left_low = halves(left)
    right_high, right_low = halves(right)
    dot = lambda a, b: jnp.dot(a, b, preferred_element_type=jnp.float32)
    return dot(left_high, right_high) + (dot(left_high, right_low) + dot(left_low, right_high))


def filter_one(i, orb, low, high, prev, pot, mat, out, ext, half, rowsum):
    planes = orb.shape[1]
    tiles = orb.shape[2] // LANES
    span = 3 * planes
    low_tiles = unpacked(low, i, 2)
    high_tiles = unpacked(high, i, 0)
    lane = lax.broadcasted_iota(jnp.int32, (planes, LANES), 1)
    rolled = None
    first = None
    for t in range(tiles):
        tile = orb[i, :, t * LANES : (t + 1) * LANES]
        ext[span * t : span * t + planes, :] = low_tiles[t]
        ext[span * t + planes : span * t + 2 * planes, :] = tile
        ext[span * t + 2 * planes : span * t + 3 * planes, :] = high_tiles[t]
        now = pltpu.roll(tile, ROW, 1)
        if t:
            half[(t - 1) * planes : t * planes, :] = jnp.where(lane < ROW, rolled, now)
        else:
            first = now
        rolled = now
    half[(tiles - 1) * planes : tiles * planes, :] = jnp.where(lane < ROW, rolled, first)
    cells = jnp.concatenate([orb[i, :, t * LANES : (t + 1) * LANES] for t in range(tiles)], axis=0)
    rowsum[...] = three_pass(cells, mat[...])
    for t in range(tiles):
        base = span * t + planes
        centre = orb[i, :, t * LANES : (t + 1) * LANES]

        def flat(step):
            u = (t + step) % tiles
            return orb[i, :, u * LANES : (u + 1) * LANES]

        def odd(step):
            u = (t + step) % tiles
            return half[u * planes : (u + 1) * planes, :]

        total = rowsum[t * planes : (t + 1) * planes, :]
        for k in range(1, 7):
            pair = ext[base + k : base + k + planes, :] + ext[base - k : base - k + planes, :]
            if k % 2:
                pair = pair + (odd((k - 1) // 2) + odd(-(k + 1) // 2))
            else:
                pair = pair + (flat(k // 2) + flat(-(k // 2)))
            total = total + np.float32(SCALE * coefs[k]) * pair
        diag = pot[:, t * LANES : (t + 1) * LANES] * np.float32(1 / 14.0) + np.float32(3 * SCALE * coefs[0] - 36.0 / 14.0)
        out[i, :, t * LANES : (t + 1) * LANES] = total + diag * centre - prev[i, :, t * LANES : (t + 1) * LANES]


def filter_body(orb, low, high, prev, pot, mat, *rest):
    @pl.loop(0, orb.shape[0])
    def _(i):
        filter_one(i, orb, low, high, prev, pot, mat, *rest[-4:])


def apply_filter(orb, low, high, prev, pot, first=0, n=None, side=0, out=0, into=None, total=None):
    planes, cells = orb.shape[1:]
    n = n or low.shape[0]
    total = total or orb.shape[0]
    tiles = cells // LANES
    thin = cells * WIDTH // planes
    step = split(n, first, side, out)
    block = lambda start, width: pl.BlockSpec((step, planes, width), lambda i: (i + start // step, 0, 0))
    args = [orb, low, high, prev, pot, jnp.asarray(row_matrix())]
    specs = [
        block(first, cells),
        block(side, thin),
        block(side, thin),
        block(first, cells),
        pl.BlockSpec((planes, cells), lambda i: (0, 0)),
        pl.BlockSpec((LANES, LANES), lambda i: (0, 0)),
    ]
    if into is not None:
        args.append(into)
        specs.append(pl.BlockSpec(memory_space=pl.ANY))
    return pl.pallas_call(
        filter_body,
        grid=(n // step,),
        in_specs=specs,
        out_specs=block(out, cells),
        out_shape=jax.ShapeDtypeStruct((total, planes, cells), jnp.float32),
        input_output_aliases={} if into is None else {6: 0},
        scratch_shapes=[
            pltpu.VMEM((tiles * 3 * planes, LANES), jnp.float32),
            pltpu.VMEM((tiles * planes, LANES), jnp.float32),
            pltpu.VMEM((tiles * planes, LANES), jnp.float32),
        ],
        compiler_params=room(14),
        cost_estimate=pl.CostEstimate(
            flops=n * planes * cells * 1600, bytes_accessed=19 * n * planes * cells, transcendentals=0
        ),
    )(*args)


def weights_body(scalars, rows, plan, high, low):
    z, core, first = scalars[0], scalars[1], scalars[2]
    offset, which, other = plan[0:1, :], plan[1:2, :], plan[2:3, :]
    seat_core = jnp.where(other == 1, 1 - core, core)
    share = plan[3:4, :]
    order = first + ((z + offset) & (RING - 1)) * share + which + seat_core * (RING * share)
    count, span = rows.shape
    columns = order.shape[1]
    planes = high.shape[0] // count
    pick = lax.broadcasted_iota(jnp.int32, (span, columns), 0) == order
    wide = jnp.dot(rows[...], pick.astype(jnp.float32), precision=lax.Precision.HIGHEST, preferred_element_type=jnp.float32)
    row = lax.broadcasted_iota(jnp.int32, (planes, columns), 0)
    col = lax.broadcasted_iota(jnp.int32, (planes, columns), 1)
    same = (col & (planes - 1)) == row
    for j in range(count):
        full = jnp.where(same, wide[j : j + 1, :], 0.0)
        top = full.astype(jnp.bfloat16).astype(jnp.float32)
        high[j * planes : (j + 1) * planes, :] = top
        low[j * planes : (j + 1) * planes, :] = full - top


def weights(rotation, plan, z, core, chip, share, planes):
    turned = rotation.T
    count = turned.shape[0]
    panel = CORES * RING * share
    per = LANES // panel
    table = np.repeat(np.asarray([(o, i, c, share) for o, i, c in plan], np.int32).T, planes, axis=1)
    table = np.concatenate([table, np.zeros((8 - table.shape[0], table.shape[1]), np.int32)])
    scalars = jnp.stack([z, core, (chip % per) * panel, chip // per])
    shape = (count * planes, table.shape[1])
    return pl.pallas_call(
        weights_body,
        grid_spec=pltpu.PrefetchScalarGridSpec(
            num_scalar_prefetch=1,
            grid=(1,),
            in_specs=[
                pl.BlockSpec((count, LANES), lambda i, s: (0, s[3])),
                pl.BlockSpec(table.shape, lambda i, s: (0, 0)),
            ],
            out_specs=[pl.BlockSpec(shape, lambda i, s: (0, 0))] * 2,
        ),
        out_shape=[jax.ShapeDtypeStruct(shape, jnp.float32)] * 2,
        compiler_params=room(6),
        cost_estimate=pl.CostEstimate(flops=10**6, bytes_accessed=10**6, transcendentals=0),
    )(scalars, turned, jnp.asarray(table))


def panel_body(acc, *rest):
    blocks, (high, low, out) = rest[:-3], rest[-3:]
    n, planes, width = acc.shape
    block = jnp.concatenate([b[...].reshape(b.shape[0] * planes, width) for b in blocks], axis=0)
    block_high = block.astype(jnp.bfloat16)
    block_low = (block - block_high.astype(jnp.float32)).astype(jnp.bfloat16)
    high = high[...].astype(jnp.bfloat16)
    low = low[...].astype(jnp.bfloat16)
    dot = lambda a, b: jnp.dot(a, b, preferred_element_type=jnp.float32)
    prod = dot(high, block_high) + (dot(high, block_low) + dot(low, block_high))
    out[...] = acc[...] + prod.reshape(n, planes, width)


def add_panel(acc, blocks, high, low):
    n, planes, cells = acc.shape
    chunk = cells // 4
    spec = lambda m: pl.BlockSpec((m, planes, chunk), lambda i: (0, 0, i))
    k = sum(b.shape[0] for b in blocks)
    full = pl.BlockSpec(high.shape, lambda i: (0, 0))
    return pl.pallas_call(
        panel_body,
        grid=(cells // chunk,),
        in_specs=[spec(n)] + [spec(b.shape[0]) for b in blocks] + [full, full],
        out_specs=spec(n),
        out_shape=jax.ShapeDtypeStruct(acc.shape, jnp.float32),
        compiler_params=room(20),
        cost_estimate=pl.CostEstimate(
            flops=6 * n * planes * planes * k * cells, bytes_accessed=4 * (2 * n + k) * planes * cells, transcendentals=0
        ),
    )(acc, *blocks, high, low)


def seat(x, z, core):
    return (x * RING + z % RING) * CORES + core


def everywhere(step):
    return [
        (seat(x, z, c), seat(*step(x, z, c))) for x in range(ROWS_X) for z in range(RING) for c in range(CORES)
    ]


ONWARD = everywhere(lambda x, z, c: (x, z + 1, c))
BACK = everywhere(lambda x, z, c: (x, z - 1, c))
ACROSS = everywhere(lambda x, z, c: (1 - x, z, c))
PARTNER = everywhere(lambda x, z, c: (x, z, 1 - c))


def open_body(place, orb, head, tail, first, second, held, hand, sems):
    share, half = hand.shape[0], first.shape[0]
    start = ((place[0] + RING // 2) & (RING - 1)) * share
    step = split(held.shape[0])
    copies = [pltpu.make_async_copy(orb.at[pl.ds(start, share)], hand, sems.at[0])]
    for i in range(0, held.shape[0], step):
        part = pl.ds(i, step)
        copies.append(pltpu.make_async_copy(orb.at[part], held.at[part], sems.at[len(copies)]))
    for copy in copies:
        copy.start()
    copies[0].wait()
    first[...] = hand[:half]
    second[...] = hand[half:]
    for i, copy in enumerate(copies[1:]):
        copy.wait()

        @pl.loop(i * step, i * step + step)
        def _(m):
            pack_one(m, held, head, tail)


def opening(orb, place, early):
    n, planes, cells = orb.shape
    share = n // RING
    shapes = [(early, planes, cells * WIDTH // planes)] * 2 + [(share // 2, planes, cells)] * 2
    still = pl.BlockSpec(memory_space=pltpu.VMEM)
    return pl.pallas_call(
        open_body,
        in_specs=[pl.BlockSpec(memory_space=pltpu.SMEM), pl.BlockSpec(memory_space=pltpu.HBM)],
        out_specs=[still] * 4,
        out_shape=[jax.ShapeDtypeStruct(shape, jnp.float32) for shape in shapes],
        scratch_shapes=[
            pltpu.VMEM((early, planes, cells), jnp.float32),
            pltpu.VMEM((share, planes, cells), jnp.float32),
            pltpu.SemaphoreType.DMA((early // split(early) + 1,)),
        ],
        compiler_params=room(60),
        cost_estimate=pl.CostEstimate(flops=0, bytes_accessed=8 * n * planes * cells, transcendentals=0),
    )(place, orb)


def pick_body(place, hand_up, hand_down, up, down, out_up, out_down):
    for hand, moved, out in ((hand_up, up, out_up), (hand_down, down, out_down)):
        for m in range(out.shape[0]):
            out[m] = jnp.where(place[1] == 0, hand[m], moved[min(m, moved.shape[0] - 1)])


def pick(block, place, step, up, down):
    n, planes, cells = block.shape
    share = n // RING
    hand = lambda step: pl.BlockSpec((share, planes, cells), lambda i, s: ((s[0] + step) & (RING - 1), 0, 0))
    still = pl.BlockSpec(memory_space=pltpu.VMEM)
    return pl.pallas_call(
        pick_body,
        grid_spec=pltpu.PrefetchScalarGridSpec(
            num_scalar_prefetch=1,
            grid=(1,),
            in_specs=[hand(step), hand(RING - step), still, still],
            out_specs=[still, still],
        ),
        out_shape=[jax.ShapeDtypeStruct((share, planes, cells), jnp.float32)] * 2,
        compiler_params=room(5),
        cost_estimate=pl.CostEstimate(flops=0, bytes_accessed=24 * share * planes * cells, transcendentals=0),
    )(place, block, block, up, down)


def settle_body(place, own, up, down, piece, *ends):
    offset = place[1]
    half = own.shape[0] // 2
    for m in range(own.shape[0]):
        middle = up[m] if m < half else down[m - half]
        far = jnp.where(offset < 4, up[m], jnp.where(offset == 4, middle, down[m]))
        piece[m] = jnp.where(offset == 0, own[m], far)
    if ends:
        pack_body(piece, *ends)


def settle(block, place, up, down, packed):
    share, planes, cells = up.shape
    hand = lambda index: pl.BlockSpec((share, planes, cells), index)
    still = pl.BlockSpec(memory_space=pltpu.VMEM)
    thin = (share, planes, cells * WIDTH // planes)
    shapes = [up.shape] + [thin] * (2 if packed else 0)
    return pl.pallas_call(
        settle_body,
        grid_spec=pltpu.PrefetchScalarGridSpec(
            num_scalar_prefetch=1,
            grid=(1,),
            in_specs=[hand(lambda i, s: (s[0], 0, 0)), still, still],
            out_specs=[still] * len(shapes),
        ),
        out_shape=[jax.ShapeDtypeStruct(shape, jnp.float32) for shape in shapes],
        compiler_params=room(5),
        cost_estimate=pl.CostEstimate(flops=0, bytes_accessed=20 * share * planes * cells, transcendentals=0),
    )(place, block, up, down)


def stack_body(*refs):
    out = refs[-1]
    for i, ref in enumerate(refs[:-1]):
        out[i] = ref[0]


def stacked(blocks):
    whole = pl.BlockSpec(memory_space=pltpu.VMEM)
    shape = (len(blocks),) + blocks[0].shape[1:]
    return pl.pallas_call(
        stack_body,
        in_specs=[whole] * len(blocks),
        out_specs=whole,
        out_shape=jax.ShapeDtypeStruct(shape, jnp.float32),
        compiler_params=room(3),
        cost_estimate=pl.CostEstimate(flops=0, bytes_accessed=8 * math.prod(shape), transcendentals=0),
    )(*blocks)


def relay(block, place, packed, opposite):
    up = lax.ppermute(opposite[0], "band", ONWARD)
    down = lax.ppermute(opposite[1], "band", BACK)
    for step in (3, 2, 1):
        up, down = pick(block, place, step, up, down)
        up = lax.ppermute(up, "band", ONWARD)
        down = lax.ppermute(down, "band", BACK)
    return settle(block, place, up, down, packed)


def halo(head, tail):
    size = lax.axis_size("domain")
    low = lax.ppermute(tail, "domain", [(i, (i + 1) % size) for i in range(size)])
    high = lax.ppermute(head, "domain", [((i + 1) % size, i) for i in range(size)])
    return low, high


def step(orbitals, previous, potential, rotation, accumulated, panel):
    count = orbitals.shape[0]
    share = count // RING
    where = lax.axis_index("band")
    x, z, core = where >> 4, (where >> 1) & 7, where & 1
    chip = panel[0] & (ROWS_X * RING - 1)
    root_x, root_z = chip >> 3, chip & 7

    offset = (z - root_z) & (RING - 1)

    early = count * 9 // 16
    place = jnp.stack([z, offset])
    *ends, first, second = opening(orbitals, place, early)
    sides_early = halo(*ends)
    ends = pack(orbitals, early, count - early)
    sides_late = halo(*ends)

    piece, *ends = relay(orbitals, place, True, (first, second))
    start = ((z + RING // 2) & (RING - 1)) * share
    size = (share // 2,) + previous.shape[1:]
    opposite = [lax.dynamic_slice(previous, (start + m * size[0], 0, 0), size) for m in range(2)]
    (before,) = relay(previous, place, False, opposite)
    below, above = halo(*ends)
    filtered = apply_filter(orbitals, *sides_early, previous, potential)
    filtered = apply_filter(orbitals, *sides_late, previous, potential, early, out=early, into=filtered)

    chains = []
    for m in range(share):
        mine = apply_filter(piece, below, above, before, potential, m, 1, m, total=1)
        other = lax.ppermute(mine, "band", ACROSS)
        chains.append([jnp.where(x == root_x, mine, other)] * 2)
    rounds = [[(chain[0], 0, m) for m, chain in enumerate(chains)]]
    for hop in range(1, RING // 2 + 1):
        rounds.append([])
        for m, chain in enumerate(chains):
            for way, pairs in enumerate((ONWARD, BACK)):
                if hop == RING // 2 and way != m % 2:
                    continue
                chain[way] = lax.ppermute(chain[way], "band", pairs)
                rounds[-1].append((chain[way], hop if way else -hop, m))
    rounds[:2] = [rounds[0] + rounds[1]]
    mine, theirs, plan = [], [], []
    for arrived in rounds:
        mine += [block for block, _, _ in arrived]
        plan += [(off, m) for _, off, m in arrived]
        group = stacked([block for block, _, _ in arrived])
        theirs.append(lax.ppermute(group, "band", PARTNER))
    blocks = mine + theirs
    plan = [(o, i, c) for c in range(CORES) for o, i in plan]
    coefficients = weights(rotation, plan, z, core, chip, share, orbitals.shape[1])
    rotated = add_panel(accumulated, blocks, *coefficients)
    return filtered, rotated


def solution(mesh):
    in_specs = (
        P("band", "domain", None),
        P("band", "domain", None),
        P("domain", None),
        P(None, "band"),
        P("band", "domain", None),
        P(),
    )
    out_specs = (P("band", "domain", None), P("band", "domain", None))
    return jax.shard_map(step, mesh=mesh, in_specs=in_specs, out_specs=out_specs, check_vma=False)
```

```python
import math

import numpy as np
import jax
import jax.numpy as jnp
from jax import lax
from jax.experimental import pallas as pl
from jax.experimental.pallas import tpu as pltpu
from jax.sharding import PartitionSpec as P


coefs = (
    -5369.0 / 1800.0,
    12.0 / 7.0,
    -15.0 / 56.0,
    10.0 / 189.0,
    -1.0 / 112.0,
    2.0 / 1925.0,
    -1.0 / 16632.0,
)
SCALE = -2.0 / 14.0
ROW = 64
LANES = 128
WIDTH = 6
ROWS_X = 2
RING = 8
CORES = 2


def split(*counts):
    return max(d for d in range(1, 6) if math.gcd(*counts) % d == 0)


def room(mib):
    return pltpu.CompilerParams(vmem_limit_bytes=mib << 20)


def row_matrix():
    out = np.zeros((LANES, LANES))
    for i in range(LANES):
        base = i - i % ROW
        for k in range(1, 7):
            for s in (k, -k):
                out[base + (i + s) % ROW, i] += SCALE * coefs[k]
    return out.astype(np.float32)


def mixed(full, spare, limit, below):
    sub = lax.broadcasted_iota(jnp.int32, full.shape, 0)
    return jnp.where(sub < limit, full, spare) if below else jnp.where(sub >= limit, full, spare)


def pack_one(i, orb, head, tail):
    for g in range(orb.shape[2] // (4 * LANES)):
        tiles = [orb[i, :, (4 * g + m) * LANES : (4 * g + m + 1) * LANES] for m in range(4)]
        for m in range(3):
            spare = pltpu.roll(tiles[3], 6 - 2 * m, 0)
            span = slice((3 * g + m) * LANES, (3 * g + m + 1) * LANES)
            head[i, :, span] = mixed(tiles[m], spare, WIDTH, True)
            tail[i, :, span] = mixed(tiles[m], spare, 2, False)


def pack_body(orb, head, tail):
    @pl.loop(0, head.shape[0])
    def _(i):
        pack_one(i, orb, head, tail)


def unpacked(side, i, first):
    out = []
    for g in range(side.shape[2] // (3 * LANES)):
        three = [side[i, :, (3 * g + m) * LANES : (3 * g + m + 1) * LANES] for m in range(3)]
        rolled = [pltpu.roll(v, 2 + 2 * m, 0) for m, v in enumerate(three)]
        last = mixed(rolled[0], mixed(rolled[1], rolled[2], first + 4, True), first + 2, True)
        out += three + [last]
    return out


def pack(orb, first=0, n=None):
    n = n or orb.shape[0]
    planes, cells = orb.shape[1:]
    thin = cells * WIDTH // planes
    step = split(n, first)
    return pl.pallas_call(
        pack_body,
        grid=(n // step,),
        in_specs=[pl.BlockSpec((step, planes, cells), lambda i: (i + first // step, 0, 0))],
        out_specs=[pl.BlockSpec((step, planes, thin), lambda i: (i, 0, 0))] * 2,
        out_shape=[jax.ShapeDtypeStruct((n, planes, thin), jnp.float32)] * 2,
        compiler_params=room(8),
        cost_estimate=pl.CostEstimate(flops=0, bytes_accessed=10 * n * planes * cells, transcendentals=0),
    )(orb)


def halves(values):
    high = values.astype(jnp.bfloat16)
    return high, (values - high.astype(jnp.float32)).astype(jnp.bfloat16)


def three_pass(left, right):
    left_high, left_low = halves(left)
    right_high, right_low = halves(right)
    dot = lambda a, b: jnp.dot(a, b, preferred_element_type=jnp.float32)
    return dot(left_high, right_high) + (dot(left_high, right_low) + dot(left_low, right_high))


def filter_one(i, orb, low, high, prev, pot, mat, out, ext, half, rowsum):
    planes = orb.shape[1]
    tiles = orb.shape[2] // LANES
    span = 3 * planes
    low_tiles = unpacked(low, i, 2)
    high_tiles = unpacked(high, i, 0)
    lane = lax.broadcasted_iota(jnp.int32, (planes, LANES), 1)
    rolled = None
    first = None
    for t in range(tiles):
        tile = orb[i, :, t * LANES : (t + 1) * LANES]
        ext[span * t : span * t + planes, :] = low_tiles[t]
        ext[span * t + planes : span * t + 2 * planes, :] = tile
        ext[span * t + 2 * planes : span * t + 3 * planes, :] = high_tiles[t]
        now = pltpu.roll(tile, ROW, 1)
        if t:
            half[(t - 1) * planes : t * planes, :] = jnp.where(lane < ROW, rolled, now)
        else:
            first = now
        rolled = now
    half[(tiles - 1) * planes : tiles * planes, :] = jnp.where(lane < ROW, rolled, first)
    cells = jnp.concatenate([orb[i, :, t * LANES : (t + 1) * LANES] for t in range(tiles)], axis=0)
    rowsum[...] = three_pass(cells, mat[...])
    for t in range(tiles):
        base = span * t + planes
        centre = orb[i, :, t * LANES : (t + 1) * LANES]

        def flat(step):
            u = (t + step) % tiles
            return orb[i, :, u * LANES : (u + 1) * LANES]

        def odd(step):
            u = (t + step) % tiles
            return half[u * planes : (u + 1) * planes, :]

        total = rowsum[t * planes : (t + 1) * planes, :]
        for k in range(1, 7):
            pair = ext[base + k : base + k + planes, :] + ext[base - k : base - k + planes, :]
            if k % 2:
                pair = pair + (odd((k - 1) // 2) + odd(-(k + 1) // 2))
            else:
                pair = pair + (flat(k // 2) + flat(-(k // 2)))
            total = total + np.float32(SCALE * coefs[k]) * pair
        diag = pot[:, t * LANES : (t + 1) * LANES] * np.float32(1 / 14.0) + np.float32(3 * SCALE * coefs[0] - 36.0 / 14.0)
        out[i, :, t * LANES : (t + 1) * LANES] = total + diag * centre - prev[i, :, t * LANES : (t + 1) * LANES]


def filter_body(orb, low, high, prev, pot, mat, *rest):
    @pl.loop(0, orb.shape[0])
    def _(i):
        filter_one(i, orb, low, high, prev, pot, mat, *rest[-4:])


def apply_filter(orb, low, high, prev, pot, first=0, n=None, side=0, out=0, into=None, total=None):
    planes, cells = orb.shape[1:]
    n = n or low.shape[0]
    total = total or orb.shape[0]
    tiles = cells // LANES
    thin = cells * WIDTH // planes
    step = split(n, first, side, out)
    block = lambda start, width: pl.BlockSpec((step, planes, width), lambda i: (i + start // step, 0, 0))
    args = [orb, low, high, prev, pot, jnp.asarray(row_matrix())]
    specs = [
        block(first, cells),
        block(side, thin),
        block(side, thin),
        block(first, cells),
        pl.BlockSpec((planes, cells), lambda i: (0, 0)),
        pl.BlockSpec((LANES, LANES), lambda i: (0, 0)),
    ]
    if into is not None:
        args.append(into)
        specs.append(pl.BlockSpec(memory_space=pl.ANY))
    return pl.pallas_call(
        filter_body,
        grid=(n // step,),
        in_specs=specs,
        out_specs=block(out, cells),
        out_shape=jax.ShapeDtypeStruct((total, planes, cells), jnp.float32),
        input_output_aliases={} if into is None else {6: 0},
        scratch_shapes=[
            pltpu.VMEM((tiles * 3 * planes, LANES), jnp.float32),
            pltpu.VMEM((tiles * planes, LANES), jnp.float32),
            pltpu.VMEM((tiles * planes, LANES), jnp.float32),
        ],
        compiler_params=room(14),
        cost_estimate=pl.CostEstimate(
            flops=n * planes * cells * 1600, bytes_accessed=19 * n * planes * cells, transcendentals=0
        ),
    )(*args)


def weights_body(scalars, rows, plan, high, low):
    z, core, first = scalars[0], scalars[1], scalars[2]
    offset, which, other = plan[0:1, :], plan[1:2, :], plan[2:3, :]
    seat_core = jnp.where(other == 1, 1 - core, core)
    share = plan[3:4, :]
    order = first + ((z + offset) & (RING - 1)) * share + which + seat_core * (RING * share)
    count, span = rows.shape
    columns = order.shape[1]
    planes = high.shape[0] // count
    pick = lax.broadcasted_iota(jnp.int32, (span, columns), 0) == order
    wide = jnp.dot(rows[...], pick.astype(jnp.float32), precision=lax.Precision.HIGHEST, preferred_element_type=jnp.float32)
    row = lax.broadcasted_iota(jnp.int32, (planes, columns), 0)
    col = lax.broadcasted_iota(jnp.int32, (planes, columns), 1)
    same = (col & (planes - 1)) == row
    for j in range(count):
        full = jnp.where(same, wide[j : j + 1, :], 0.0)
        top = full.astype(jnp.bfloat16).astype(jnp.float32)
        high[j * planes : (j + 1) * planes, :] = top
        low[j * planes : (j + 1) * planes, :] = full - top


def weights(rotation, plan, z, core, chip, share, planes):
    turned = rotation.T
    count = turned.shape[0]
    panel = CORES * RING * share
    per = LANES // panel
    table = np.repeat(np.asarray([(o, i, c, share) for o, i, c in plan], np.int32).T, planes, axis=1)
    table = np.concatenate([table, np.zeros((8 - table.shape[0], table.shape[1]), np.int32)])
    scalars = jnp.stack([z, core, (chip % per) * panel, chip // per])
    shape = (count * planes, table.shape[1])
    return pl.pallas_call(
        weights_body,
        grid_spec=pltpu.PrefetchScalarGridSpec(
            num_scalar_prefetch=1,
            grid=(1,),
            in_specs=[
                pl.BlockSpec((count, LANES), lambda i, s: (0, s[3])),
                pl.BlockSpec(table.shape, lambda i, s: (0, 0)),
            ],
            out_specs=[pl.BlockSpec(shape, lambda i, s: (0, 0))] * 2,
        ),
        out_shape=[jax.ShapeDtypeStruct(shape, jnp.float32)] * 2,
        compiler_params=room(6),
        cost_estimate=pl.CostEstimate(flops=10**6, bytes_accessed=10**6, transcendentals=0),
    )(scalars, turned, jnp.asarray(table))


def panel_body(acc, *rest):
    blocks, (high, low, out) = rest[:-3], rest[-3:]
    n, planes, width = acc.shape
    block = jnp.concatenate([b[...].reshape(b.shape[0] * planes, width) for b in blocks], axis=0)
    block_high = block.astype(jnp.bfloat16)
    block_low = (block - block_high.astype(jnp.float32)).astype(jnp.bfloat16)
    high = high[...].astype(jnp.bfloat16)
    low = low[...].astype(jnp.bfloat16)
    dot = lambda a, b: jnp.dot(a, b, preferred_element_type=jnp.float32)
    prod = dot(high, block_high) + (dot(high, block_low) + dot(low, block_high))
    out[...] = acc[...] + prod.reshape(n, planes, width)


def add_panel(acc, blocks, high, low):
    n, planes, cells = acc.shape
    chunk = cells // 4
    spec = lambda m: pl.BlockSpec((m, planes, chunk), lambda i: (0, 0, i))
    k = sum(b.shape[0] for b in blocks)
    full = pl.BlockSpec(high.shape, lambda i: (0, 0))
    return pl.pallas_call(
        panel_body,
        grid=(cells // chunk,),
        in_specs=[spec(n)] + [spec(b.shape[0]) for b in blocks] + [full, full],
        out_specs=spec(n),
        out_shape=jax.ShapeDtypeStruct(acc.shape, jnp.float32),
        compiler_params=room(20),
        cost_estimate=pl.CostEstimate(
            flops=6 * n * planes * planes * k * cells, bytes_accessed=4 * (2 * n + k) * planes * cells, transcendentals=0
        ),
    )(acc, *blocks, high, low)


def seat(x, z, core):
    return (x * RING + z % RING) * CORES + core


def everywhere(step):
    return [
        (seat(x, z, c), seat(*step(x, z, c))) for x in range(ROWS_X) for z in range(RING) for c in range(CORES)
    ]


ONWARD = everywhere(lambda x, z, c: (x, z + 1, c))
BACK = everywhere(lambda x, z, c: (x, z - 1, c))
ACROSS = everywhere(lambda x, z, c: (1 - x, z, c))
PARTNER = everywhere(lambda x, z, c: (x, z, 1 - c))


def open_body(place, orb, head, tail, first, second):
    share = orb.shape[0] // RING
    start = ((place[0] + RING // 2) & (RING - 1)) * share
    for m in range(first.shape[0]):
        first[m] = orb[start + m]
        second[m] = orb[start + first.shape[0] + m]
    pack_body(orb, head, tail)


def opening(orb, place, early):
    n, planes, cells = orb.shape
    half = n // RING // 2
    shapes = [(early, planes, cells * WIDTH // planes)] * 2 + [(half, planes, cells)] * 2
    still = pl.BlockSpec(memory_space=pltpu.VMEM)
    return pl.pallas_call(
        open_body,
        in_specs=[pl.BlockSpec(memory_space=pltpu.SMEM), still],
        out_specs=[still] * 4,
        out_shape=[jax.ShapeDtypeStruct(shape, jnp.float32) for shape in shapes],
        compiler_params=room(12),
        cost_estimate=pl.CostEstimate(flops=0, bytes_accessed=8 * n * planes * cells, transcendentals=0),
    )(place, orb)


def pick_body(place, hand_up, hand_down, up, down, out_up, out_down):
    for hand, moved, out in ((hand_up, up, out_up), (hand_down, down, out_down)):
        for m in range(out.shape[0]):
            out[m] = jnp.where(place[1] == 0, hand[m], moved[min(m, moved.shape[0] - 1)])


def pick(block, place, step, up, down):
    n, planes, cells = block.shape
    share = n // RING
    hand = lambda step: pl.BlockSpec((share, planes, cells), lambda i, s: ((s[0] + step) & (RING - 1), 0, 0))
    still = pl.BlockSpec(memory_space=pltpu.VMEM)
    return pl.pallas_call(
        pick_body,
        grid_spec=pltpu.PrefetchScalarGridSpec(
            num_scalar_prefetch=1,
            grid=(1,),
            in_specs=[hand(step), hand(RING - step), still, still],
            out_specs=[still, still],
        ),
        out_shape=[jax.ShapeDtypeStruct((share, planes, cells), jnp.float32)] * 2,
        compiler_params=room(5),
        cost_estimate=pl.CostEstimate(flops=0, bytes_accessed=24 * share * planes * cells, transcendentals=0),
    )(place, block, block, up, down)


def settle_body(place, own, up, down, piece, *ends):
    offset = place[1]
    half = own.shape[0] // 2
    for m in range(own.shape[0]):
        middle = up[m] if m < half else down[m - half]
        far = jnp.where(offset < 4, up[m], jnp.where(offset == 4, middle, down[m]))
        piece[m] = jnp.where(offset == 0, own[m], far)
    if ends:
        pack_body(piece, *ends)


def settle(block, place, up, down, packed):
    share, planes, cells = up.shape
    hand = lambda index: pl.BlockSpec((share, planes, cells), index)
    still = pl.BlockSpec(memory_space=pltpu.VMEM)
    thin = (share, planes, cells * WIDTH // planes)
    shapes = [up.shape] + [thin] * (2 if packed else 0)
    return pl.pallas_call(
        settle_body,
        grid_spec=pltpu.PrefetchScalarGridSpec(
            num_scalar_prefetch=1,
            grid=(1,),
            in_specs=[hand(lambda i, s: (s[0], 0, 0)), still, still],
            out_specs=[still] * len(shapes),
        ),
        out_shape=[jax.ShapeDtypeStruct(shape, jnp.float32) for shape in shapes],
        compiler_params=room(5),
        cost_estimate=pl.CostEstimate(flops=0, bytes_accessed=20 * share * planes * cells, transcendentals=0),
    )(place, block, up, down)


def stack_body(*refs):
    out = refs[-1]
    for i, ref in enumerate(refs[:-1]):
        out[i] = ref[0]


def stacked(blocks):
    whole = pl.BlockSpec(memory_space=pltpu.VMEM)
    shape = (len(blocks),) + blocks[0].shape[1:]
    return pl.pallas_call(
        stack_body,
        in_specs=[whole] * len(blocks),
        out_specs=whole,
        out_shape=jax.ShapeDtypeStruct(shape, jnp.float32),
        compiler_params=room(3),
        cost_estimate=pl.CostEstimate(flops=0, bytes_accessed=8 * math.prod(shape), transcendentals=0),
    )(*blocks)


def relay(block, place, packed, opposite):
    up = lax.ppermute(opposite[0], "band", ONWARD)
    down = lax.ppermute(opposite[1], "band", BACK)
    for step in (3, 2, 1):
        up, down = pick(block, place, step, up, down)
        up = lax.ppermute(up, "band", ONWARD)
        down = lax.ppermute(down, "band", BACK)
    return settle(block, place, up, down, packed)


def halo(head, tail):
    size = lax.axis_size("domain")
    low = lax.ppermute(tail, "domain", [(i, (i + 1) % size) for i in range(size)])
    high = lax.ppermute(head, "domain", [((i + 1) % size, i) for i in range(size)])
    return low, high


def step(orbitals, previous, potential, rotation, accumulated, panel):
    count = orbitals.shape[0]
    share = count // RING
    where = lax.axis_index("band")
    x, z, core = where >> 4, (where >> 1) & 7, where & 1
    chip = panel[0] & (ROWS_X * RING - 1)
    root_x, root_z = chip >> 3, chip & 7

    offset = (z - root_z) & (RING - 1)

    early = count * 5 // 8
    place = jnp.stack([z, offset])
    *ends, first, second = opening(orbitals, z[None], early)
    sides_early = halo(*ends)
    ends = pack(orbitals, early, count - early)
    sides_late = halo(*ends)

    piece, *ends = relay(orbitals, place, True, (first, second))
    start = ((z + RING // 2) & (RING - 1)) * share
    size = (share // 2,) + previous.shape[1:]
    opposite = [lax.dynamic_slice(previous, (start + m * size[0], 0, 0), size) for m in range(2)]
    (before,) = relay(previous, place, False, opposite)
    below, above = halo(*ends)
    filtered = apply_filter(orbitals, *sides_early, previous, potential)
    filtered = apply_filter(orbitals, *sides_late, previous, potential, early, out=early, into=filtered)

    chains = []
    for m in range(share):
        mine = apply_filter(piece, below, above, before, potential, m, 1, m, total=1)
        other = lax.ppermute(mine, "band", ACROSS)
        chains.append([jnp.where(x == root_x, mine, other)] * 2)
    rounds = [[(chain[0], 0, m) for m, chain in enumerate(chains)]]
    for hop in range(1, RING // 2 + 1):
        rounds.append([])
        for m, chain in enumerate(chains):
            for way, pairs in enumerate((ONWARD, BACK)):
                if hop == RING // 2 and way != m % 2:
                    continue
                chain[way] = lax.ppermute(chain[way], "band", pairs)
                rounds[-1].append((chain[way], hop if way else -hop, m))
    rounds[:2] = [rounds[0] + rounds[1]]
    mine, theirs, plan = [], [], []
    for arrived in rounds:
        mine += [block for block, _, _ in arrived]
        plan += [(off, m) for _, off, m in arrived]
        group = stacked([block for block, _, _ in arrived])
        theirs.append(lax.ppermute(group, "band", PARTNER))
    blocks = mine + theirs
    plan = [(o, i, c) for c in range(CORES) for o, i in plan]
    coefficients = weights(rotation, plan, z, core, chip, share, orbitals.shape[1])
    rotated = add_panel(accumulated, blocks, *coefficients)
    return filtered, rotated


def solution(mesh):
    in_specs = (
        P("band", "domain", None),
        P("band", "domain", None),
        P("domain", None),
        P(None, "band"),
        P("band", "domain", None),
        P(),
    )
    out_specs = (P("band", "domain", None), P("band", "domain", None))
    return jax.shard_map(step, mesh=mesh, in_specs=in_specs, out_specs=out_specs, check_vma=False)
```
